768 devices in a mesh: dp: 64 (over y, z_hi, x), space: 12 (over z_lo, core).
Axes of the slice: x: 4, y: 8, z: 12 (z_hi: 2, z_lo: 6; z = z_hi * 6 + z_lo), core: 2. Of those that a mesh axis runs over, the one named last changes fastest.
Arguments:
- features: bfloat16 [64, 72, 32, 1024], P('dp', 'space'), may hold values from -6 to 6
- labels: int32 [64, 72, 32], P('dp', 'space'), may hold values from 0 to 2
- pixel_weight: int32 [64, 72, 32], P('dp', 'space'), may hold values from 1 to 4
- conv_weight: bfloat16 [1024, 9, 128], replicated, may hold values from -0.0625 to 0.0625
- conv_bias: float32 [128], replicated, may hold values from -3 to 3
- class_weight: bfloat16 [128, 3], replicated, may hold values from -1.5 to 1.5
Outputs:
- features_grad: float32 [64, 72, 32, 1024], P('dp', 'space')
- weight_grad: float32 [9216, 128], P(('dp', 'space'))
The draws below stay inside these ranges and needn't reach their ends.
All inputs are finite; a program needn't handle non-finite values.
Results may differ from the reference program's by a relative error of at most 0.011.
Values may be sent and summed in bfloat16 or wider, within the bound.
A program may use at most 64 MiB of HBM per device.

```python
import jax
import jax.numpy as jnp
from jax import lax

CIN = 1024
COUT = 128
NCLS = 3
TAPS = 9
DILATION_SIZE = 6
COLS = 32
NIMG = 64
HEIGHT = 72


def place_ends(result, stream_key, smallest, high):
    dims = result.shape
    index_at = [jax.random.randint(jax.random.fold_in(stream_key, axis), (), 0, dims[axis]) for axis in range(len(dims))]
    result = result.at[tuple(index_at)].set(smallest)
    longest = dims.index(max(dims))
    index_at[longest] = (index_at[longest] + 1) % dims[longest]
    return result.at[tuple(index_at)].set(high)


def steps_of(key, dims, shards, smallest, largest):
    gain, own = 1.0, jax.random.fold_in(key, 6)
    for axis_at, parts in shards:
        heights = jnp.exp(jax.random.uniform(jax.random.fold_in(own, axis_at), (parts,), jnp.float32, smallest / len(shards), largest / len(shards)))
        gain = gain * jnp.repeat(heights, dims[axis_at] // parts).reshape([-1 if axis == axis_at else 1 for axis in range(len(dims))])
    return gain


def noise(stream_key, shape, spread, limit, split=(), kind=jnp.bfloat16):
    array = spread * jax.random.normal(stream_key, shape, jnp.float32)
    if split:
        array = array * steps_of(stream_key, shape, split, -0.22, 0.18)
    return jnp.clip(array, -limit, limit).astype(kind)


def setup_inputs(seed: int = 0) -> dict:
    splits = jax.random.split(jax.random.key(seed), 7)
    return {
        "features": noise(splits[0], (NIMG, HEIGHT, COLS, CIN), 1.0, 6.0, ((0, 64), (1, 12))),
        "labels": place_ends(jax.random.randint(splits[1], (NIMG, HEIGHT, COLS), 0, NCLS), jax.random.fold_in(splits[1], 1), 0, NCLS - 1).astype(jnp.int32),
        "pixel_weight": place_ends(jax.random.randint(splits[2], (NIMG, HEIGHT, COLS), 1, 5), jax.random.fold_in(splits[2], 1), 1, 4).astype(jnp.int32),
        "conv_weight": noise(splits[3], (CIN, TAPS, COUT), (CIN * TAPS) ** -0.5, 0.0625),
        "conv_bias": noise(splits[4], (COUT,), 0.5, 3.0, (), jnp.float32),
        "class_weight": noise(splits[5], (COUT, NCLS), 0.25, 1.5),
    }


def one_image(conv_weight, conv_bias, class_weight, input_image, label_map, weight_map):
    image_height, image_width, input_width = input_image.shape
    output_width = conv_weight.shape[2]
    pixel_count = image_height * image_width
    padded_input = jnp.pad(input_image, ((DILATION_SIZE, DILATION_SIZE), (DILATION_SIZE, DILATION_SIZE), (0, 0)))
    preact = jnp.zeros((pixel_count, output_width), jnp.float32)
    for tap_row in range(3):
        for column_tap in range(3):
            input_piece = padded_input[tap_row * DILATION_SIZE:tap_row * DILATION_SIZE + image_height, column_tap * DILATION_SIZE:column_tap * DILATION_SIZE + image_width].reshape(pixel_count, input_width)
            preact = preact + jnp.dot(input_piece, conv_weight[:, 3 * tap_row + column_tap, :], preferred_element_type=jnp.float32)
    preact = preact + conv_bias
    sigmoid_z = jax.nn.sigmoid(preact)
    hidden = (preact * sigmoid_z).astype(jnp.bfloat16)
    logits = jnp.dot(hidden, class_weight, preferred_element_type=jnp.float32)
    exponent = jnp.exp(logits)
    chances = exponent / jnp.sum(exponent, axis=1, keepdims=True)
    classes = jnp.arange(NCLS, dtype=jnp.int32)[None, :]
    onehot = (label_map.reshape(pixel_count, 1) == classes).astype(jnp.float32)
    grad_logits = weight_map.reshape(pixel_count, 1).astype(jnp.float32) * (chances - onehot)
    hidden_grad = jnp.dot(grad_logits, class_weight.astype(jnp.float32).T, precision=lax.Precision.HIGHEST)
    preact_gradient = (hidden_grad * sigmoid_z * (1.0 + preact * (1.0 - sigmoid_z))).astype(jnp.bfloat16)
    padded_gradient = jnp.pad(preact_gradient.reshape(image_height, image_width, output_width), ((DILATION_SIZE, DILATION_SIZE), (DILATION_SIZE, DILATION_SIZE), (0, 0)))
    flat_image = input_image.reshape(pixel_count, input_width)
    feature_grad = jnp.zeros((pixel_count, input_width), jnp.float32)
    tap_grads = []
    for tap_row in range(3):
        for column_tap in range(3):
            upper_row = (2 - tap_row) * DILATION_SIZE
            left_column = (2 - column_tap) * DILATION_SIZE
            input_piece = padded_gradient[upper_row:upper_row + image_height, left_column:left_column + image_width].reshape(pixel_count, output_width)
            feature_grad = feature_grad + lax.dot_general(input_piece, conv_weight[:, 3 * tap_row + column_tap, :], (((1,), (1,)), ((), ())), preferred_element_type=jnp.float32)
            tap_grads.append(lax.dot_general(flat_image, input_piece, (((0,), (0,)), ((), ())), preferred_element_type=jnp.float32))
    return feature_grad.reshape(image_height, image_width, input_width), jnp.stack(tap_grads, axis=1)


def reference(features, labels, pixel_weight, conv_weight, conv_bias, class_weight):
    def image_step(carry, inputs):
        input_image, label_map, weight_map = inputs
        feature_grad, kernel_grad = one_image(conv_weight, conv_bias, class_weight, input_image, label_map, weight_map)
        return carry + kernel_grad, feature_grad

    initial = jnp.zeros(conv_weight.shape, jnp.float32)
    summed, features_grad = lax.scan(image_step, initial, (features, labels, pixel_weight))
    weight_grad = (summed / NIMG).reshape(conv_weight.shape[0] * conv_weight.shape[1], conv_weight.shape[2])
    return features_grad, weight_grad
```

```python
import jax
import jax.numpy as jnp
from jax import lax
from jax.experimental import pallas as pl
from jax.experimental.pallas import tpu as pltpu
from jax.sharding import PartitionSpec as P

MESH = pl.DeviceIdType.MESH
F32 = jnp.float32
BF16 = jnp.bfloat16

ROWS, COLS, CIN, COUT, NCLS = 6, 32, 1024, 128, 3
SHIFT = 6
PIX = ROWS * COLS
HALF = CIN // 2
NX, NY, NZ, NZL = 4, 8, 12, 6
BANDS = 2 * NZL
IMAGES = 64


def step_kernel(
    f_hbm, w_hbm, lab_ref, pw_ref, bias_ref, cwt_ref,
    fg_hbm, wg_ref,
    fv, wv, other, ft, cwp, qs, rq, gs, con, rx, cy, ry, pz, cz, rz, fg,
    load_sem, out_sem, qs_sem, rq_sem, fs_sem, fr_sem, gsend_sem, grecv_sem,
    xs_sem, xr_sem, ys_sem, yr_sem, zs_sem, zr_sem,
):
    dp = lax.axis_index("dp")
    space = lax.axis_index("space")
    x = lax.rem(dp, 4)
    zh = lax.rem(lax.div(dp, 4), 2)
    y = lax.div(dp, 8)
    core = lax.rem(space, 2)
    zl = lax.div(space, 2)
    yhalf = lax.div(y, 4)

    def dev(yy, hh, xx, ss):
        return ((yy * 2 + hh) * 4 + xx, ss)

    loads = [pltpu.make_async_copy(f_hbm, fv, load_sem.at[0])]
    for n, a in enumerate((0, 2, 1)):
        loads.append(
            pltpu.make_async_copy(w_hbm.at[pl.ds(3 * a, 3)], wv.at[pl.ds(3 * a, 3)], load_sem.at[1 + n])
        )
    for c in loads:
        c.start()

    barrier = pltpu.get_barrier_semaphore()

    def greet(device):
        pl.semaphore_signal(barrier, inc=1, device_id=device, device_id_type=MESH)

    partner = (dp, zl * 2 + 1 - core)
    greet(partner)
    for k in range(1, NX):
        greet(dev(y, zh, lax.rem(x + k, NX), space))

    @pl.when(zl > 0)
    def _():
        greet((dp, zl * 2 - 1))

    @pl.when(zl < NZL - 1)
    def _():
        greet((dp, zl * 2 + 2))

    for k in range(NY):
        @pl.when(jnp.logical_or(core != yhalf, y != k))
        def _():
            greet(dev(k, zh, x, zl * 2 + yhalf))

    for h in range(2):
        for l in range(NZL):
            @pl.when(jnp.logical_or(core != zh, jnp.logical_or(zh != h, zl != l)))
            def _():
                greet(dev(y, h, x, l * 2 + zh))

    near = jnp.where(core == 0, jnp.where(zl > 0, 2, 0), jnp.where(zl < NZL - 1, 2, 0))
    expected = (
        1 + 3 + near + (8 - jnp.where(core == yhalf, 1, 0)) + (12 - jnp.where(core == zh, 1, 0))
    )

    column = lax.rem(lax.broadcasted_iota(jnp.int32, (PIX, COUT), 0), COLS)
    has_left = column >= SHIFT
    has_right = column < COLS - SHIFT

    def from_left(v):
        return jnp.where(has_left, pltpu.roll(v, SHIFT, 0), 0.0)

    def from_right(v):
        return jnp.where(has_right, pltpu.roll(v, PIX - SHIFT, 0), 0.0)

    def partial(a):
        wa = jnp.concatenate([wv[3 * a + b] for b in range(3)], axis=1)
        p = jnp.dot(fv[...], wa, preferred_element_type=F32)
        return (
            p[:, COUT : 2 * COUT]
            + from_left(p[:, :COUT])
            + from_right(p[:, 2 * COUT :])
        )

    @pl.when(space == 0)
    def _():
        rq[0] = jnp.zeros((PIX, COUT), F32)

    @pl.when(space == BANDS - 1)
    def _():
        rq[1] = jnp.zeros((PIX, COUT), F32)

    @pl.when(zl == 0)
    def _():
        gs[1, pl.ds(0, PIX)] = jnp.zeros((PIX, COUT), BF16)

    @pl.when(zl == NZL - 1)
    def _():
        gs[1, pl.ds(3 * PIX, PIX)] = jnp.zeros((PIX, COUT), BF16)

    cwp[...] = jnp.zeros((COUT, COUT), F32)
    cwp[pl.ds(0, NCLS), :] = cwt_ref[...].astype(F32)
    pz[pl.ds(144, 16), :] = jnp.zeros((16, COUT), F32)

    loads[0].wait()
    loads[1].wait()
    qs[0] = partial(0)
    loads[2].wait()
    qs[1] = partial(2)
    pl.semaphore_wait(barrier, expected)

    up = pltpu.make_async_remote_copy(
        qs.at[0], rq.at[0], qs_sem.at[0], rq_sem.at[0],
        device_id=(dp, lax.rem(space + 1, BANDS)), device_id_type=MESH)
    down = pltpu.make_async_remote_copy(
        qs.at[1], rq.at[1], qs_sem.at[1], rq_sem.at[1],
        device_id=(dp, lax.rem(space + BANDS - 1, BANDS)), device_id_type=MESH)

    @pl.when(space < BANDS - 1)
    def _():
        up.start()

    @pl.when(space > 0)
    def _():
        down.start()

    swap = pltpu.make_async_remote_copy(
        fv.at[:, pl.ds(pl.multiple_of((1 - core) * HALF, HALF), HALF)], other,
        fs_sem, fr_sem, device_id=partner, device_id_type=MESH)
    swap.start()

    loads[3].wait()
    local = partial(1) + bias_ref[...]
    ft[core] = fv[:, pl.ds(pl.multiple_of(core * HALF, HALF), HALF)].T

    eye = (
        lax.broadcasted_iota(jnp.int32, (COLS, COLS), 0)
        == lax.broadcasted_iota(jnp.int32, (COLS, COLS), 1)
    )

    def per_pixel(ref):
        return jnp.concatenate(
            [
                jnp.sum(
                    jnp.where(eye, jnp.broadcast_to(ref[r].astype(F32), (COLS, COLS)), 0.0),
                    axis=1, keepdims=True,
                )
                for r in range(ROWS)
            ],
            axis=0,
        )

    label = per_pixel(lab_ref)
    weight = per_pixel(pw_ref)

    @pl.when(space > 0)
    def _():
        up.wait_recv()

    @pl.when(space < BANDS - 1)
    def _():
        down.wait_recv()

    preact = local + rq[0] + rq[1]
    sig = jax.nn.sigmoid(preact)
    hidden = (preact * sig).astype(BF16)
    proj = cwp[...]
    logits = lax.dot_general(
        hidden, proj.astype(BF16), (((1,), (1,)), ((), ())), preferred_element_type=F32)
    lane = lax.broadcasted_iota(jnp.int32, (PIX, COUT), 1)
    real = lane < NCLS
    expo = jnp.where(real, jnp.exp(logits), 0.0)
    chances = expo / jnp.sum(expo, axis=1, keepdims=True)
    onehot = jnp.where(lane.astype(F32) == label, 1.0, 0.0)
    grad_logits = jnp.where(real, weight * (chances - onehot), 0.0)
    hidden_grad = lax.dot_general(
        grad_logits, proj, (((1,), (0,)), ((), ())),
        precision=lax.Precision.HIGHEST, preferred_element_type=F32)
    grad = hidden_grad * sig * (1.0 + preact * (1.0 - sig))
    mine = pl.multiple_of((1 + core) * PIX, PIX)
    gs[1, pl.ds(mine, PIX)] = grad.astype(BF16)

    to_partner = pltpu.make_async_remote_copy(
        gs.at[1, pl.ds(mine, PIX)], gs.at[1, pl.ds(mine, PIX)],
        gsend_sem.at[0], grecv_sem.at[0], device_id=partner, device_id_type=MESH)
    to_partner.start()
    far = pl.multiple_of((1 - core) * 3 * PIX, PIX)
    next_zl = lax.rem(zl + jnp.where(core == 0, NZL - 1, 1), NZL)
    has_next = near > 0
    to_near = [
        pltpu.make_async_remote_copy(
            gs.at[1, pl.ds(mine, PIX)], gs.at[1, pl.ds(far, PIX)],
            gsend_sem.at[1 + k], grecv_sem.at[2 - core],
            device_id=(dp, next_zl * 2 + k), device_id_type=MESH)
        for k in range(2)
    ]

    @pl.when(has_next)
    def _():
        for c in to_near:
            c.start()

    def spread(start):
        g = gs[1, pl.ds(start, PIX)].astype(F32)
        gs[0, pl.ds(start, PIX)] = from_right(g).astype(BF16)
        gs[2, pl.ds(start, PIX)] = from_left(g).astype(BF16)

    spread(mine)
    swap.wait_recv()
    ft[1 - core] = other[...].T
    theirs = pl.multiple_of((2 - core) * PIX, PIX)
    from_partner = pltpu.make_async_remote_copy(
        gs.at[1, pl.ds(theirs, PIX)], gs.at[1, pl.ds(theirs, PIX)],
        gsend_sem.at[0], grecv_sem.at[0], device_id=partner, device_id_type=MESH)
    from_partner.wait_recv()
    spread(theirs)

    def x_copy(a, k):
        to = lax.rem(x + k, NX)
        return pltpu.make_async_remote_copy(
            con.at[a, to], rx.at[a, k - 1], xs_sem.at[a, k - 1], xr_sem.at[a, k - 1],
            device_id=dev(y, zh, to, space), device_id_type=MESH)

    def contribute(a):
        total = None
        for q in range(2):
            rhs = jnp.concatenate(
                [gs[b, pl.ds((2 - a + q) * PIX, PIX)] for b in range(3)], axis=1)
            part = jnp.dot(ft[q], rhs, preferred_element_type=F32)
            total = part if total is None else total + part
        total = total.astype(BF16)
        for m in range(HALF // 16):
            yz, xd = divmod(m, NX)
            for b in range(3):
                con[a, xd, pl.ds((yz * 3 + b) * 16, 16), :] = total[
                    m * 16 : (m + 1) * 16, b * COUT : (b + 1) * COUT]
        for k in (2, 1, 3):
            x_copy(a, k).start()

    contribute(1)

    @pl.when(zl > 0)
    def _():
        pltpu.make_async_remote_copy(
            gs.at[1, pl.ds(0, PIX)], gs.at[1, pl.ds(0, PIX)],
            gsend_sem.at[0], grecv_sem.at[1], device_id=partner, device_id_type=MESH).wait_recv()

    @pl.when(zl < NZL - 1)
    def _():
        pltpu.make_async_remote_copy(
            gs.at[1, pl.ds(3 * PIX, PIX)], gs.at[1, pl.ds(3 * PIX, PIX)],
            gsend_sem.at[0], grecv_sem.at[2], device_id=partner, device_id_type=MESH).wait_recv()

    spread(3 * PIX)
    contribute(0)
    spread(0)
    contribute(2)

    cols = jnp.concatenate(
        [
            gs[b, pl.ds(pl.multiple_of((core + 2 - a) * PIX, PIX), PIX)]
            for a in range(3)
            for b in range(3)
        ],
        axis=1,
    )
    outs = []
    for n in range(4):
        width = CIN // 4
        wn = jnp.concatenate([wv[t, pl.ds(n * width, width)] for t in range(9)], axis=1)
        fg[:, pl.ds(n * width, width)] = lax.dot_general(
            cols, wn, (((1,), (1,)), ((), ())), preferred_element_type=F32)
        outs.append(
            pltpu.make_async_copy(
                fg.at[:, pl.ds(n * width, width)], fg_hbm.at[:, pl.ds(n * width, width)],
                out_sem.at[n]))
        outs[-1].start()

    def y_target(yz):
        return dev(core * 4 + yz // 2, zh, x, zl * 2 + yz % 2)

    def y_remote(a, yz):
        return pltpu.make_async_remote_copy(
            cy.at[a, pl.ds(yz * 48, 48)], ry.at[a, y], ys_sem.at[a, yz], yr_sem.at[a, y],
            device_id=y_target(yz), device_id_type=MESH)

    def y_is_self(yz):
        return jnp.logical_and(y == core * 4 + yz // 2, core == yz % 2)

    for a in (1, 0, 2):
        for k in (2, 1, 3):
            x_copy(a, k).wait_recv()
        total = con[a, x].astype(F32)
        for k in range(3):
            total = total + rx[a, k].astype(F32)
        cy[a] = total.astype(BF16)
        for yz in range(8):
            itself = y_is_self(yz)

            @pl.when(itself)
            def _():
                pltpu.make_async_copy(
                    cy.at[a, pl.ds(yz * 48, 48)], ry.at[a, y], yr_sem.at[a, y]).start()

            @pl.when(jnp.logical_not(itself))
            def _():
                y_remote(a, yz).start()

    for a in (1, 0, 2):
        total = None
        for k in range(NY):
            pltpu.make_async_copy(
                cy.at[a, pl.ds(0, 48)], ry.at[a, k], yr_sem.at[a, k]).wait()
            part = ry[a, k].astype(F32)
            total = part if total is None else total + part
        for b in range(3):
            pz[pl.ds(3 * a + b, 16, stride=9), :] = total[b * 16 : (b + 1) * 16]

    z = zh * NZL + zl
    z_self = [jnp.logical_and(core == zh, space == s) for s in range(BANDS)]

    def z_remote(s):
        return pltpu.make_async_remote_copy(
            cz.at[s], rz.at[z], zs_sem.at[s], zr_sem.at[z],
            device_id=dev(y, core, x, s), device_id_type=MESH)

    for s in range(BANDS):
        cz[s] = pz[pl.ds(12 * s, 16), :].astype(BF16)
    for s in range(BANDS):
        @pl.when(z_self[s])
        def _():
            pltpu.make_async_copy(cz.at[s], rz.at[z], zr_sem.at[z]).start()

        @pl.when(jnp.logical_not(z_self[s]))
        def _():
            z_remote(s).start()

    total = None
    for k in range(NZ):
        pltpu.make_async_copy(cz.at[0], rz.at[k], zr_sem.at[k]).wait()
        part = rz[k].astype(F32)
        total = part if total is None else total + part
    wg_ref[...] = total[:12] / IMAGES

    for c in outs:
        c.wait()

    @pl.when(space < BANDS - 1)
    def _():
        up.wait_send()

    @pl.when(space > 0)
    def _():
        down.wait_send()

    swap.wait_send()
    to_partner.wait_send()

    @pl.when(has_next)
    def _():
        for c in to_near:
            c.wait_send()

    for a in range(3):
        for k in range(1, NX):
            x_copy(a, k).wait_send()
        for yz in range(8):
            @pl.when(jnp.logical_not(y_is_self(yz)))
            def _():
                y_remote(a, yz).wait_send()

    for s in range(BANDS):
        @pl.when(jnp.logical_not(z_self[s]))
        def _():
            z_remote(s).wait_send()


def on_device(features, labels, pixel_weight, conv_weight, conv_bias, class_weight):
    image = features.reshape(PIX, CIN)
    taps = conv_weight.transpose(1, 0, 2)
    vmem = pl.BlockSpec(memory_space=pltpu.VMEM)
    hbm = pl.BlockSpec(memory_space=pl.ANY)
    dma = pltpu.SemaphoreType.DMA
    feature_grad, weight_grad = pl.pallas_call(
        step_kernel,
        out_shape=(
            jax.ShapeDtypeStruct((PIX, CIN), F32),
            jax.ShapeDtypeStruct((12, COUT), F32),
        ),
        in_specs=[hbm, hbm, vmem, vmem, vmem, vmem],
        out_specs=(hbm, vmem),
        scratch_shapes=[
            pltpu.VMEM((PIX, CIN), BF16),
            pltpu.VMEM((9, CIN, COUT), BF16),
            pltpu.VMEM((PIX, HALF), BF16),
            pltpu.VMEM((2, HALF, PIX), BF16),
            pltpu.VMEM((COUT, COUT), F32),
            pltpu.VMEM((2, PIX, COUT), F32),
            pltpu.VMEM((2, PIX, COUT), F32),
            pltpu.VMEM((3, 4 * PIX, COUT), BF16),
            pltpu.VMEM((3, NX, 384, COUT), BF16),
            pltpu.VMEM((3, NX - 1, 384, COUT), BF16),
            pltpu.VMEM((3, 384, COUT), BF16),
            pltpu.VMEM((3, NY, 48, COUT), BF16),
            pltpu.VMEM((160, COUT), F32),
            pltpu.VMEM((BANDS, 16, COUT), BF16),
            pltpu.VMEM((NZ, 16, COUT), BF16),
            pltpu.VMEM((PIX, CIN), F32),
            dma((4,)), dma((4,)), dma((2,)), dma((2,)), dma, dma, dma((3,)), dma((3,)),
            dma((3, 3)), dma((3, 3)), dma((3, 8)), dma((3, 8)), dma((BANDS,)), dma((NZ,)),
        ],
        compiler_params=pltpu.CompilerParams(
            collective_id=0, has_side_effects=True, vmem_limit_bytes=60 * 1024 * 1024),
        name="step",
    )(
        image, taps, labels.transpose(1, 0, 2), pixel_weight.transpose(1, 0, 2),
        conv_bias.reshape(1, COUT), class_weight.T,
    )
    return feature_grad.reshape(features.shape), weight_grad


def solution(mesh):
    placed = (
        P("dp", "space", None, None),
        P("dp", "space", None),
        P("dp", "space", None),
        P(),
        P(),
        P(),
    )
    return jax.shard_map(
        on_device,
        mesh=mesh,
        in_specs=placed,
        out_specs=(P("dp", "space", None, None), P(("dp", "space"), None)),
        check_vma=False,
    )
```

```python
import jax
import jax.numpy as jnp
from jax import lax
from jax.experimental import pallas as pl
from jax.experimental.pallas import tpu as pltpu
from jax.sharding import PartitionSpec as P

MESH = pl.DeviceIdType.MESH
F32 = jnp.float32
BF16 = jnp.bfloat16

ROWS, COLS, CIN, COUT, NCLS = 6, 32, 1024, 128, 3
SHIFT = 6
PIX = ROWS * COLS
QUARTER = CIN // 4
NX, NY = 4, 8
BANDS = 12
NSRC = 6
IMAGES = 64
WRITES = 8
VMEM_LIMIT = 60 * 1024 * 1024


def step_kernel(
    f_hbm, w_hbm, lab_hbm, pw_hbm, bias_hbm, cwt_hbm,
    fg_hbm, rz,
    fv, wv, lab_ref, pw_ref, bias_ref, cwt_ref,
    quarter, cwp, qs, rq, gs, con, rx, cy, ry, pz, cz, fg,
    load_sem, out_sem, qs_sem, rq_sem, fs_sem, fr_sem, gs_sem, gh_sem, gr_sem,
    xs_sem, xr_sem, ys_sem, yr_sem, zs_sem, zr_sem,
):
    dp = lax.axis_index("dp")
    space = lax.axis_index("space")
    x = lax.rem(dp, NX)
    zh = lax.rem(lax.div(dp, NX), 2)
    y = lax.div(dp, 2 * NX)
    core = lax.rem(space, 2)
    zl = lax.div(space, 2)
    q = lax.rem(space, 4)
    m = lax.div(space, 4)
    odd = lax.rem(zl, 2)
    share = 2 * core + odd
    home = lax.div(y, 2)
    active = odd == lax.rem(home, 2)

    def dev(yy, hh, xx, ss):
        return ((yy * 2 + hh) * NX + xx, ss)

    def send(src, dst, send_sem, recv_sem, device):
        return pltpu.make_async_remote_copy(
            src, dst, send_sem, recv_sem, device_id=device, device_id_type=MESH)

    def arrived(dst, sem):
        pltpu.make_async_copy(dst, dst, sem).wait()

    loads = [pltpu.make_async_copy(f_hbm, fv, load_sem.at[0])]
    for n, a in enumerate((0, 2, 1)):
        loads.append(
            pltpu.make_async_copy(w_hbm.at[pl.ds(3 * a, 3)], wv.at[pl.ds(3 * a, 3)], load_sem.at[1 + n]))
    small = [
        pltpu.make_async_copy(src, dst, load_sem.at[4 + n])
        for n, (src, dst) in enumerate(
            ((cwt_hbm, cwt_ref), (bias_hbm, bias_ref), (lab_hbm, lab_ref), (pw_hbm, pw_ref)))
    ]
    for c in loads + small:
        c.start()

    barrier = pltpu.get_barrier_semaphore()

    def greet(device):
        pl.semaphore_signal(barrier, inc=1, device_id=device, device_id_type=MESH)

    for k in range(1, 4):
        greet((dp, 4 * m + lax.rem(q + k, 4)))
    for k in range(1, NX):
        greet(dev(y, zh, lax.rem(x + k, NX), space))

    @pl.when(m > 0)
    def _():
        greet((dp, 4 * m - 1))

    @pl.when(m < 2)
    def _():
        greet((dp, 4 * m + 4))

    for k in range(NY):
        @pl.when(jnp.logical_and(active, jnp.logical_or(share != home, y != k)))
        def _():
            greet(dev(k, zh, x, zl * 2 + lax.div(y, 4)))

    z_mine = jnp.logical_and(active, core == zh)
    slot = zh * 3 + m
    for j in range(NSRC):
        @pl.when(jnp.logical_not(jnp.logical_and(z_mine, slot == j)))
        def _():
            greet(dev(y, j // 3, x, (2 * (j % 3) + lax.rem(home, 2)) * 2 + zh))

    lower = jnp.logical_and(q == 0, m > 0)
    upper = jnp.logical_and(q == 3, m < 2)
    edge = jnp.logical_or(lower, upper)
    expected = (
        3 + jnp.where(edge, 4, 0) + 3 + (4 - jnp.where(share == home, 1, 0))
        + jnp.where(active, 12 - jnp.where(core == zh, 1, 0), 0)
    )

    column = lax.rem(lax.broadcasted_iota(jnp.int32, (PIX, COUT), 0), COLS)
    has_left = column >= SHIFT
    has_right = column < COLS - SHIFT

    def from_left(v):
        return jnp.where(has_left, pltpu.roll(v, SHIFT, 0), 0.0)

    def from_right(v):
        return jnp.where(has_right, pltpu.roll(v, PIX - SHIFT, 0), 0.0)

    def gather_taps(p):
        return p[:, COUT : 2 * COUT] + from_left(p[:, :COUT]) + from_right(p[:, 2 * COUT : 3 * COUT])

    def products(rows):
        w = jnp.concatenate([wv[3 * a + b] for a in rows for b in range(3)], axis=1)
        return jnp.dot(fv[...], w, preferred_element_type=F32)

    @pl.when(space == 0)
    def _():
        rq[0] = jnp.zeros((PIX, COUT), F32)
        gs[1, pl.ds(0, PIX)] = jnp.zeros((PIX, COUT), BF16)

    @pl.when(space == BANDS - 1)
    def _():
        rq[1] = jnp.zeros((PIX, COUT), F32)

    @pl.when(jnp.logical_and(m == 0, space != 0))
    def _():
        gs[1, pl.ds(0, PIX)] = jnp.zeros((PIX, COUT), BF16)

    @pl.when(m == 2)
    def _():
        gs[1, pl.ds(5 * PIX, PIX)] = jnp.zeros((PIX, COUT), BF16)

    cwp[...] = jnp.zeros((COUT, COUT), F32)
    pz[pl.ds(144, 16), :] = jnp.zeros((16, COUT), F32)

    loads[0].wait()
    loads[1].wait()
    loads[2].wait()
    both = products((0, 2))
    qs[0] = gather_taps(both[:, : 3 * COUT])
    qs[1] = gather_taps(both[:, 3 * COUT :])
    pl.semaphore_wait(barrier, expected)

    up = send(qs.at[0], rq.at[0], qs_sem.at[0], rq_sem.at[0], (dp, lax.rem(space + 1, BANDS)))
    down = send(qs.at[1], rq.at[1], qs_sem.at[1], rq_sem.at[1], (dp, lax.rem(space + BANDS - 1, BANDS)))

    @pl.when(space < BANDS - 1)
    def _():
        up.start()

    @pl.when(space > 0)
    def _():
        down.start()

    def band_of(k):
        return pl.ds(k * PIX, PIX)

    def quarter_copy(k):
        return send(
            fv.at[:, pl.ds((2 * (k % 2) + k // 2) * QUARTER, QUARTER)],
            quarter.at[pl.ds(pl.multiple_of(q * PIX, PIX), PIX)],
            fs_sem.at[k], fr_sem.at[q], (dp, 4 * m + k))

    for k in range(4):
        @pl.when(q != k)
        def _():
            quarter_copy(k).start()

        @pl.when(q == k)
        def _():
            pltpu.make_async_copy(
                fv.at[:, pl.ds((2 * (k % 2) + k // 2) * QUARTER, QUARTER)],
                quarter.at[band_of(k)], fr_sem.at[q]).start()

    loads[3].wait()
    for c in small:
        c.wait()
    cwp[pl.ds(0, NCLS), :] = cwt_ref[...].astype(F32)
    local = gather_taps(products((1,))) + bias_ref[...]

    eye = (
        lax.broadcasted_iota(jnp.int32, (COLS, COLS), 0)
        == lax.broadcasted_iota(jnp.int32, (COLS, COLS), 1)
    )

    def per_pixel(ref):
        return jnp.concatenate(
            [
                jnp.sum(
                    jnp.where(eye, jnp.broadcast_to(ref[r].astype(F32), (COLS, COLS)), 0.0),
                    axis=1, keepdims=True,
                )
                for r in range(ROWS)
            ],
            axis=0,
        )

    label = per_pixel(lab_ref)
    weight = per_pixel(pw_ref)

    @pl.when(space > 0)
    def _():
        up.wait_recv()

    @pl.when(space < BANDS - 1)
    def _():
        down.wait_recv()

    preact = local + rq[0] + rq[1]
    sig = jax.nn.sigmoid(preact)
    hidden = (preact * sig).astype(BF16)
    proj = cwp[...]
    logits = lax.dot_general(
        hidden, proj.astype(BF16), (((1,), (1,)), ((), ())), preferred_element_type=F32)
    lane = lax.broadcasted_iota(jnp.int32, (PIX, COUT), 1)
    real = lane < NCLS
    expo = jnp.where(real, jnp.exp(logits), 0.0)
    chances = expo / jnp.sum(expo, axis=1, keepdims=True)
    onehot = jnp.where(lane.astype(F32) == label, 1.0, 0.0)
    grad_logits = jnp.where(real, weight * (chances - onehot), 0.0)
    hidden_grad = lax.dot_general(
        grad_logits, proj, (((1,), (0,)), ((), ())),
        precision=lax.Precision.HIGHEST, preferred_element_type=F32)
    grad = hidden_grad * sig * (1.0 + preact * (1.0 - sig))

    def window(w):
        return pl.ds(pl.multiple_of(w * PIX, PIX), PIX)

    mine = window(q + 1)
    gs[1, mine] = grad.astype(BF16)
    for k in range(1, 4):
        send(gs.at[1, mine], gs.at[1, mine], gs_sem.at[k - 1], gr_sem.at[q + 1],
             (dp, 4 * m + lax.rem(q + k, 4))).start()

    def halo_copy(k):
        return send(
            gs.at[1, mine], gs.at[1, window(jnp.where(q == 0, 5, 0))],
            gh_sem.at[k], gr_sem.at[jnp.where(q == 0, 5, 0)],
            (dp, lax.rem(4 * (m + jnp.where(q == 0, 2, 1)), BANDS) + k))

    @pl.when(edge)
    def _():
        for k in range(4):
            halo_copy(k).start()

    def spread(w):
        g = gs[1, window(w)].astype(F32)
        gs[0, window(w)] = from_right(g).astype(BF16)
        gs[2, window(w)] = from_left(g).astype(BF16)

    spread(q + 1)
    for k in range(4):
        arrived(quarter.at[band_of(k)], fr_sem.at[k])
    columns = quarter[...].T
    for k in range(1, 4):
        w = 1 + lax.rem(q + k, 4)
        arrived(gs.at[1, window(w)], gr_sem.at[w])
        spread(w)

    def x_copy(a, k):
        to = lax.rem(x + k, NX)
        return send(
            con.at[a, to], rx.at[a, k - 1], xs_sem.at[a, k - 1], xr_sem.at[a, k - 1],
            dev(y, zh, to, space))

    def contribute(a):
        rhs = jnp.concatenate(
            [gs[b, pl.ds((2 - a) * PIX, 4 * PIX)] for b in range(3)], axis=1)
        total = jnp.dot(columns, rhs, preferred_element_type=F32).astype(BF16)
        for n in range(QUARTER // 16):
            yz, xd = divmod(n, NX)
            for b in range(3):
                con[a, xd, pl.ds((yz * 3 + b) * 16, 16), :] = total[
                    n * 16 : (n + 1) * 16, b * COUT : (b + 1) * COUT]
        for k in (2, 1, 3):
            x_copy(a, k).start()

    contribute(1)

    @pl.when(m < 2)
    def _():
        arrived(gs.at[1, window(5)], gr_sem.at[5])

    spread(5)
    contribute(0)

    @pl.when(m > 0)
    def _():
        arrived(gs.at[1, window(0)], gr_sem.at[0])

    spread(0)
    contribute(2)

    around = jnp.concatenate(
        [gs[b, window(q + 2 - a)] for a in range(3) for b in range(3)], axis=1)
    outs = []
    for n in range(4):
        width = CIN // 4
        wn = jnp.concatenate([wv[t, pl.ds(n * width, width)] for t in range(9)], axis=1)
        fg[:, pl.ds(n * width, width)] = lax.dot_general(
            around, wn, (((1,), (1,)), ((), ())), preferred_element_type=F32)
        outs.append(
            pltpu.make_async_copy(
                fg.at[:, pl.ds(n * width, width)], fg_hbm.at[:, pl.ds(n * width, width)],
                out_sem.at[n]))
        outs[-1].start()

    def y_target(yz):
        return dev(2 * share + yz // 2, zh, x, zl * 2 + yz % 2)

    def y_copy(a, yz):
        return send(
            cy.at[a, pl.ds(yz * 48, 48)], ry.at[a, y], ys_sem.at[a, yz], yr_sem.at[a, y],
            y_target(yz))

    def y_is_self(yz):
        return jnp.logical_and(y == 2 * share + yz // 2, core == yz % 2)

    for a in (1, 0, 2):
        for k in (2, 1, 3):
            x_copy(a, k).wait_recv()
        total = con[a, x].astype(F32)
        for k in range(3):
            total = total + rx[a, k].astype(F32)
        cy[a] = total.astype(BF16)
        for yz in range(4):
            itself = y_is_self(yz)

            @pl.when(itself)
            def _():
                pltpu.make_async_copy(
                    cy.at[a, pl.ds(yz * 48, 48)], ry.at[a, y], yr_sem.at[a, y]).start()

            @pl.when(jnp.logical_not(itself))
            def _():
                y_copy(a, yz).start()

    def z_copy(s):
        return send(cz.at[s], rz.at[slot], zs_sem.at[s], zr_sem.at[slot], dev(y, core, x, s))

    def z_is_self(s):
        return jnp.logical_and(core == zh, space == s)

    @pl.when(active)
    def _():
        for a in (1, 0, 2):
            total = None
            for k in range(NY):
                arrived(ry.at[a, k], yr_sem.at[a, k])
                part = ry[a, k].astype(F32)
                total = part if total is None else total + part
            for b in range(3):
                pz[pl.ds(3 * a + b, 16, stride=9), :] = total[b * 16 : (b + 1) * 16]
        for s in range(BANDS):
            cz[s] = pz[pl.ds(12 * s, 16), :].astype(BF16)
        for s in range(BANDS):
            @pl.when(z_is_self(s))
            def _():
                pltpu.make_async_copy(cz.at[s], rz.at[slot], zr_sem.at[slot]).start()

            @pl.when(jnp.logical_not(z_is_self(s)))
            def _():
                z_copy(s).start()

    for c in outs:
        c.wait()

    @pl.when(space < BANDS - 1)
    def _():
        up.wait_send()

    @pl.when(space > 0)
    def _():
        down.wait_send()

    for k in range(4):
        @pl.when(q != k)
        def _():
            quarter_copy(k).wait_send()

    for k in range(1, 4):
        send(gs.at[1, mine], gs.at[1, mine], gs_sem.at[k - 1], gr_sem.at[q + 1],
             (dp, 4 * m + lax.rem(q + k, 4))).wait_send()

    @pl.when(edge)
    def _():
        for k in range(4):
            halo_copy(k).wait_send()

    for a in range(3):
        for k in range(1, NX):
            x_copy(a, k).wait_send()
        for yz in range(4):
            @pl.when(jnp.logical_not(y_is_self(yz)))
            def _():
                y_copy(a, yz).wait_send()

    @pl.when(active)
    def _():
        for s in range(BANDS):
            @pl.when(jnp.logical_not(z_is_self(s)))
            def _():
                z_copy(s).wait_send()

    for j in range(NSRC):
        arrived(rz.at[j], zr_sem.at[j])


def write_kernel(fg_in, rz_in, fg_out, wg_out, fg, rz, wg, in_sem, out_sem):
    parts = WRITES
    rows = PIX // parts
    first = pltpu.make_async_copy(rz_in, rz, in_sem.at[parts])
    first.start()
    copies = []
    for n in range(parts):
        at = pl.ds(n * rows, rows)
        copies.append((
            pltpu.make_async_copy(fg_in.at[at], fg.at[at], in_sem.at[n]),
            pltpu.make_async_copy(fg.at[at], fg_out.at[at], out_sem.at[n]),
        ))
        copies[-1][0].start()
    first.wait()
    total = rz[0].astype(F32)
    for j in range(1, NSRC):
        total = total + rz[j].astype(F32)
    wg[...] = total[:12] / IMAGES
    last = pltpu.make_async_copy(wg, wg_out, out_sem.at[parts])
    last.start()
    for load, store in copies:
        load.wait()
        store.start()
    for load, store in copies:
        store.wait()
    last.wait()


def on_device(features, labels, pixel_weight, conv_weight, conv_bias, class_weight):
    image = features.reshape(PIX, CIN)
    taps = conv_weight.transpose(1, 0, 2)
    hbm = pl.BlockSpec(memory_space=pltpu.HBM)
    dma = pltpu.SemaphoreType.DMA
    feature_grad, pieces = pl.pallas_call(
        step_kernel,
        out_shape=(
            jax.ShapeDtypeStruct((PIX, CIN), F32),
            jax.ShapeDtypeStruct((NSRC, 16, COUT), BF16),
        ),
        in_specs=[hbm] * 6,
        out_specs=(hbm, hbm),
        scratch_shapes=[
            pltpu.VMEM((PIX, CIN), BF16),
            pltpu.VMEM((9, CIN, COUT), BF16),
            pltpu.VMEM((ROWS, 1, COLS), jnp.int32),
            pltpu.VMEM((ROWS, 1, COLS), jnp.int32),
            pltpu.VMEM((1, COUT), F32),
            pltpu.VMEM((NCLS, COUT), BF16),
            pltpu.VMEM((4 * PIX, QUARTER), BF16),
            pltpu.VMEM((COUT, COUT), F32),
            pltpu.VMEM((2, PIX, COUT), F32),
            pltpu.VMEM((2, PIX, COUT), F32),
            pltpu.VMEM((3, 6 * PIX, COUT), BF16),
            pltpu.VMEM((3, NX, 192, COUT), BF16),
            pltpu.VMEM((3, NX - 1, 192, COUT), BF16),
            pltpu.VMEM((3, 192, COUT), BF16),
            pltpu.VMEM((3, NY, 48, COUT), BF16),
            pltpu.VMEM((160, COUT), F32),
            pltpu.VMEM((BANDS, 16, COUT), BF16),
            pltpu.VMEM((PIX, CIN), F32),
            dma((8,)), dma((4,)), dma((2,)), dma((2,)), dma((4,)), dma((4,)), dma((3,)), dma((4,)), dma((6,)),
            dma((3, 3)), dma((3, 3)), dma((3, 4)), dma((3, NY)), dma((BANDS,)), dma((NSRC,)),
        ],
        compiler_params=pltpu.CompilerParams(
            collective_id=0, has_side_effects=True, vmem_limit_bytes=VMEM_LIMIT),
        name="step",
    )(
        image, taps, labels.transpose(1, 0, 2), pixel_weight.transpose(1, 0, 2),
        conv_bias.reshape(1, COUT), class_weight.T,
    )
    feature_grad, weight_grad = pl.pallas_call(
        write_kernel,
        out_shape=(
            jax.ShapeDtypeStruct((PIX, CIN), F32),
            jax.ShapeDtypeStruct((12, COUT), F32),
        ),
        in_specs=[hbm] * 2,
        out_specs=(hbm, hbm),
        scratch_shapes=[
            pltpu.VMEM((PIX, CIN), F32),
            pltpu.VMEM((NSRC, 16, COUT), BF16),
            pltpu.VMEM((12, COUT), F32),
            dma((WRITES + 1,)), dma((WRITES + 1,)),
        ],
        compiler_params=pltpu.CompilerParams(vmem_limit_bytes=VMEM_LIMIT),
        name="write",
    )(feature_grad, pieces)
    return feature_grad.reshape(features.shape), weight_grad


def solution(mesh):
    placed = (
        P("dp", "space", None, None),
        P("dp", "space", None),
        P("dp", "space", None),
        P(),
        P(),
        P(),
    )
    return jax.shard_map(
        on_device,
        mesh=mesh,
        in_specs=placed,
        out_specs=(P("dp", "space", None, None), P(("dp", "space"), None)),
        check_vma=False,
    )
```

```python
import jax
import jax.numpy as jnp
from jax import lax
from jax.experimental import pallas as pl
from jax.experimental.pallas import tpu as pltpu
from jax.sharding import PartitionSpec as P

MESH = pl.DeviceIdType.MESH
F32 = jnp.float32
BF16 = jnp.bfloat16

ROWS, COLS, CIN, COUT, NCLS = 6, 32, 1024, 128, 3
SHIFT = 6
PIX = ROWS * COLS
QUARTER = CIN // 4
NX, NY = 4, 8
BANDS = 12
NSRC = 6
IMAGES = 64
WRITES = 8
VMEM_LIMIT = 60 * 1024 * 1024


def step_kernel(
    f_hbm, w_hbm, lab_hbm, pw_hbm, bias_hbm, cwt_hbm,
    fg_hbm, rz,
    fv, wv, lab_ref, pw_ref, bias_ref, cwt_ref,
    quarter, cwp, qs, rq, gs, con, rx, cy, ry, con1, rx1, cy1, ry1, early, early_in, late, late_in, pz, cz, fg,
    load_sem, out_sem, qs_sem, rq_sem, fs_sem, fr_sem, gs_sem, gh_sem, gr_sem,
    xs_sem, xr_sem, ys_sem, yr_sem, es_sem, er_sem, ls_sem, lr_sem, zs_sem, zr_sem,
):
    dp = lax.axis_index("dp")
    space = lax.axis_index("space")
    x = lax.rem(dp, NX)
    zh = lax.rem(lax.div(dp, NX), 2)
    y = lax.div(dp, 2 * NX)
    core = lax.rem(space, 2)
    zl = lax.div(space, 2)
    q = lax.rem(space, 4)
    m = lax.div(space, 4)
    odd = lax.rem(zl, 2)
    share = 2 * core + odd
    home = lax.div(y, 2)
    active = odd == lax.rem(home, 2)

    def dev(yy, hh, xx, ss):
        return ((yy * 2 + hh) * NX + xx, ss)

    def send(src, dst, send_sem, recv_sem, device):
        return pltpu.make_async_remote_copy(
            src, dst, send_sem, recv_sem, device_id=device, device_id_type=MESH)

    def arrived(dst, sem):
        pltpu.make_async_copy(dst, dst, sem).wait()

    loads = [pltpu.make_async_copy(f_hbm, fv, load_sem.at[0])]
    for n, a in enumerate((0, 2, 1)):
        loads.append(
            pltpu.make_async_copy(w_hbm.at[pl.ds(3 * a, 3)], wv.at[pl.ds(3 * a, 3)], load_sem.at[1 + n]))
    small = [
        pltpu.make_async_copy(src, dst, load_sem.at[4 + n])
        for n, (src, dst) in enumerate(
            ((cwt_hbm, cwt_ref), (bias_hbm, bias_ref), (lab_hbm, lab_ref), (pw_hbm, pw_ref)))
    ]
    for c in loads + small:
        c.start()

    barrier = pltpu.get_barrier_semaphore()

    def greet(device):
        pl.semaphore_signal(barrier, inc=1, device_id=device, device_id_type=MESH)

    for k in range(1, 4):
        greet((dp, 4 * m + lax.rem(q + k, 4)))
    for k in range(1, NX):
        greet(dev(y, zh, lax.rem(x + k, NX), space))

    @pl.when(m > 0)
    def _():
        greet((dp, 4 * m - 1))

    @pl.when(m < 2)
    def _():
        greet((dp, 4 * m + 4))

    for k in range(NY):
        @pl.when(jnp.logical_and(active, jnp.logical_or(share != home, y != k)))
        def _():
            greet(dev(k, zh, x, zl * 2 + lax.div(y, 4)))

    z_mine = jnp.logical_and(active, core == zh)
    slot = zh * 3 + m
    for j in range(NSRC):
        @pl.when(jnp.logical_not(jnp.logical_and(z_mine, slot == j)))
        def _():
            greet(dev(y, j // 3, x, (2 * (j % 3) + lax.rem(home, 2)) * 2 + zh))

    lower = jnp.logical_and(q == 0, m > 0)
    upper = jnp.logical_and(q == 3, m < 2)
    edge = jnp.logical_or(lower, upper)
    expected = (
        3 + jnp.where(edge, 4, 0) + 3 + (4 - jnp.where(share == home, 1, 0))
        + jnp.where(active, 12 - jnp.where(core == zh, 1, 0), 0)
    )

    column = lax.rem(lax.broadcasted_iota(jnp.int32, (PIX, COUT), 0), COLS)
    has_left = column >= SHIFT
    has_right = column < COLS - SHIFT

    def from_left(v):
        return jnp.where(has_left, pltpu.roll(v, SHIFT, 0), 0.0)

    def from_right(v):
        return jnp.where(has_right, pltpu.roll(v, PIX - SHIFT, 0), 0.0)

    def gather_taps(p):
        return p[:, COUT : 2 * COUT] + from_left(p[:, :COUT]) + from_right(p[:, 2 * COUT : 3 * COUT])

    def products(rows):
        w = jnp.concatenate([wv[3 * a + b] for a in rows for b in range(3)], axis=1)
        return jnp.dot(fv[...], w, preferred_element_type=F32)

    @pl.when(space == 0)
    def _():
        rq[0] = jnp.zeros((PIX, COUT), F32)
        gs[1, pl.ds(0, PIX)] = jnp.zeros((PIX, COUT), BF16)

    @pl.when(space == BANDS - 1)
    def _():
        rq[1] = jnp.zeros((PIX, COUT), F32)

    @pl.when(jnp.logical_and(m == 0, space != 0))
    def _():
        gs[1, pl.ds(0, PIX)] = jnp.zeros((PIX, COUT), BF16)

    @pl.when(m == 2)
    def _():
        gs[1, pl.ds(5 * PIX, PIX)] = jnp.zeros((PIX, COUT), BF16)

    cwp[...] = jnp.zeros((COUT, COUT), F32)
    pz[pl.ds(144, 16), :] = jnp.zeros((16, COUT), F32)

    loads[0].wait()
    loads[1].wait()
    loads[2].wait()
    both = products((0, 2))
    qs[0] = gather_taps(both[:, : 3 * COUT])
    qs[1] = gather_taps(both[:, 3 * COUT :])
    pl.semaphore_wait(barrier, expected)

    up = send(qs.at[0], rq.at[0], qs_sem.at[0], rq_sem.at[0], (dp, lax.rem(space + 1, BANDS)))
    down = send(qs.at[1], rq.at[1], qs_sem.at[1], rq_sem.at[1], (dp, lax.rem(space + BANDS - 1, BANDS)))

    @pl.when(space < BANDS - 1)
    def _():
        up.start()

    @pl.when(space > 0)
    def _():
        down.start()

    def band_of(k):
        return pl.ds(k * PIX, PIX)

    def quarter_copy(k):
        return send(
            fv.at[:, pl.ds((2 * (k % 2) + k // 2) * QUARTER, QUARTER)],
            quarter.at[pl.ds(pl.multiple_of(q * PIX, PIX), PIX)],
            fs_sem.at[k], fr_sem.at[q], (dp, 4 * m + k))

    for k in range(4):
        @pl.when(q != k)
        def _():
            quarter_copy(k).start()

        @pl.when(q == k)
        def _():
            pltpu.make_async_copy(
                fv.at[:, pl.ds((2 * (k % 2) + k // 2) * QUARTER, QUARTER)],
                quarter.at[band_of(k)], fr_sem.at[q]).start()

    loads[3].wait()
    for c in small:
        c.wait()
    cwp[pl.ds(0, NCLS), :] = cwt_ref[...].astype(F32)
    local = gather_taps(products((1,))) + bias_ref[...]

    eye = (
        lax.broadcasted_iota(jnp.int32, (COLS, COLS), 0)
        == lax.broadcasted_iota(jnp.int32, (COLS, COLS), 1)
    )

    def per_pixel(ref):
        return jnp.concatenate(
            [
                jnp.sum(
                    jnp.where(eye, jnp.broadcast_to(ref[r].astype(F32), (COLS, COLS)), 0.0),
                    axis=1, keepdims=True,
                )
                for r in range(ROWS)
            ],
            axis=0,
        )

    label = per_pixel(lab_ref)
    weight = per_pixel(pw_ref)

    @pl.when(space > 0)
    def _():
        up.wait_recv()

    @pl.when(space < BANDS - 1)
    def _():
        down.wait_recv()

    preact = local + rq[0] + rq[1]
    sig = jax.nn.sigmoid(preact)
    hidden = (preact * sig).astype(BF16)
    proj = cwp[...]
    logits = lax.dot_general(
        hidden, proj.astype(BF16), (((1,), (1,)), ((), ())), preferred_element_type=F32)
    lane = lax.broadcasted_iota(jnp.int32, (PIX, COUT), 1)
    real = lane < NCLS
    expo = jnp.where(real, jnp.exp(logits), 0.0)
    chances = expo / jnp.sum(expo, axis=1, keepdims=True)
    onehot = jnp.where(lane.astype(F32) == label, 1.0, 0.0)
    grad_logits = jnp.where(real, weight * (chances - onehot), 0.0)
    hidden_grad = lax.dot_general(
        grad_logits, proj, (((1,), (0,)), ((), ())),
        precision=lax.Precision.HIGHEST, preferred_element_type=F32)
    grad = hidden_grad * sig * (1.0 + preact * (1.0 - sig))

    def window(w):
        return pl.ds(pl.multiple_of(w * PIX, PIX), PIX)

    mine = window(q + 1)
    gs[1, mine] = grad.astype(BF16)
    for k in range(1, 4):
        send(gs.at[1, mine], gs.at[1, mine], gs_sem.at[k - 1], gr_sem.at[q + 1],
             (dp, 4 * m + lax.rem(q + k, 4))).start()

    def halo_copy(k):
        return send(
            gs.at[1, mine], gs.at[1, window(jnp.where(q == 0, 5, 0))],
            gh_sem.at[k], gr_sem.at[jnp.where(q == 0, 5, 0)],
            (dp, lax.rem(4 * (m + jnp.where(q == 0, 2, 1)), BANDS) + k))

    @pl.when(edge)
    def _():
        for k in range(4):
            halo_copy(k).start()

    def spread(w):
        g = gs[1, window(w)].astype(F32)
        gs[0, window(w)] = from_right(g).astype(BF16)
        gs[2, window(w)] = from_left(g).astype(BF16)

    spread(q + 1)
    for k in range(4):
        arrived(quarter.at[band_of(k)], fr_sem.at[k])
    columns = quarter[...].T
    for k in range(1, 4):
        w = 1 + lax.rem(q + k, 4)
        arrived(gs.at[1, window(w)], gr_sem.at[w])
        spread(w)

    def group(n, wide, narrow):
        return narrow if n == 0 else wide.at[n - 1]

    def group_rows(n):
        return 16 if n == 0 else 48

    def x_copy(n, k):
        to = lax.rem(x + k, NX)
        return send(
            group(n, con, con1).at[to], group(n, rx, rx1).at[k - 1],
            xs_sem.at[n, k - 1], xr_sem.at[n, k - 1], dev(y, zh, to, space))

    def y_target(yz):
        return dev(2 * share + yz // 2, zh, x, zl * 2 + yz % 2)

    def y_is_self(yz):
        return jnp.logical_and(y == 2 * share + yz // 2, core == yz % 2)

    def y_send(src, dst, send_sem, recv_sem, yz):
        itself = y_is_self(yz)

        @pl.when(itself)
        def _():
            pltpu.make_async_copy(src, dst, recv_sem).start()

        @pl.when(jnp.logical_not(itself))
        def _():
            send(src, dst, send_sem, recv_sem, y_target(yz)).start()

    def early_refs(yz):
        return early.at[yz], early_in.at[y], es_sem.at[yz], er_sem.at[y]

    def contribute(a):
        rhs = jnp.concatenate(
            [gs[b, pl.ds((2 - a) * PIX, 4 * PIX)] for b in range(3)], axis=1)
        total = jnp.dot(columns, rhs, preferred_element_type=F32).astype(BF16)
        for c in range(QUARTER // 16):
            yz, xd = divmod(c, NX)
            for b in range(3):
                piece = total[c * 16 : (c + 1) * 16, b * COUT : (b + 1) * COUT]
                if a != 1:
                    con[a // 2, xd, pl.ds((yz * 3 + b) * 16, 16), :] = piece
                elif b == 0:
                    con1[xd, pl.ds(yz * 16, 16), :] = piece
                else:
                    early[yz, pl.ds((xd * 2 + b - 1) * 16, 16), :] = piece
        for k in (2, 1, 3):
            x_copy((1, 0, 2)[a], k).start()
        if a == 1:
            for yz in range(4):
                y_send(*early_refs(yz), yz)

    contribute(1)

    @pl.when(m < 2)
    def _():
        arrived(gs.at[1, window(5)], gr_sem.at[5])

    spread(5)
    contribute(0)

    @pl.when(m > 0)
    def _():
        arrived(gs.at[1, window(0)], gr_sem.at[0])

    spread(0)
    contribute(2)

    around = jnp.concatenate(
        [gs[b, window(q + 2 - a)] for a in range(3) for b in range(3)], axis=1)
    outs = []
    for n in range(4):
        width = CIN // 4
        wn = jnp.concatenate([wv[t, pl.ds(n * width, width)] for t in range(9)], axis=1)
        fg[:, pl.ds(n * width, width)] = lax.dot_general(
            around, wn, (((1,), (1,)), ((), ())), preferred_element_type=F32)
        outs.append(
            pltpu.make_async_copy(
                fg.at[:, pl.ds(n * width, width)], fg_hbm.at[:, pl.ds(n * width, width)],
                out_sem.at[n]))
        outs[-1].start()

    def y_refs(n, yz):
        rows = group_rows(n)
        return (
            group(n, cy, cy1).at[pl.ds(yz * rows, rows)], group(n, ry, ry1).at[y],
            ys_sem.at[n, yz], yr_sem.at[n, y])

    for n in range(3):
        for k in (2, 1, 3):
            x_copy(n, k).wait_recv()
        total = group(n, con, con1)[x].astype(F32)
        for k in range(3):
            total = total + group(n, rx, rx1)[k].astype(F32)
        group(n, cy, cy1)[...] = total.astype(BF16)
        for yz in range(4):
            y_send(*y_refs(n, yz), yz)

    def late_copy(k):
        to = lax.rem(x + k, NX)
        return send(
            late.at[to], late_in.at[k - 1], ls_sem.at[k - 1], lr_sem.at[k - 1],
            dev(y, zh, to, space))

    def z_copy(s):
        return send(cz.at[s], rz.at[slot], zs_sem.at[s], zr_sem.at[slot], dev(y, core, x, s))

    def z_is_self(s):
        return jnp.logical_and(core == zh, space == s)

    @pl.when(active)
    def _():
        total = None
        for k in range(NY):
            arrived(early_in.at[k], er_sem.at[k])
            part = early_in[k].astype(F32)
            total = part if total is None else total + part
        for to in range(NX):
            late[to] = total[to * 32 : (to + 1) * 32].astype(BF16)
        for k in (2, 1, 3):
            late_copy(k).start()
        for n in range(3):
            total = None
            for k in range(NY):
                arrived(group(n, ry, ry1).at[k], yr_sem.at[n, k])
                part = group(n, ry, ry1)[k].astype(F32)
                total = part if total is None else total + part
            for b, tap in enumerate(((3,), (0, 1, 2), (6, 7, 8))[n]):
                pz[pl.ds(tap, 16, stride=9), :] = total[b * 16 : (b + 1) * 16]
        total = late[x].astype(F32)
        for k in (2, 1, 3):
            late_copy(k).wait_recv()
            total = total + late_in[k - 1].astype(F32)
        for b in range(2):
            pz[pl.ds(4 + b, 16, stride=9), :] = total[b * 16 : (b + 1) * 16]
        for s in range(BANDS):
            cz[s] = pz[pl.ds(12 * s, 16), :].astype(BF16)
        for s in range(BANDS):
            @pl.when(z_is_self(s))
            def _():
                pltpu.make_async_copy(cz.at[s], rz.at[slot], zr_sem.at[slot]).start()

            @pl.when(jnp.logical_not(z_is_self(s)))
            def _():
                z_copy(s).start()

    for c in outs:
        c.wait()

    @pl.when(space < BANDS - 1)
    def _():
        up.wait_send()

    @pl.when(space > 0)
    def _():
        down.wait_send()

    for k in range(4):
        @pl.when(q != k)
        def _():
            quarter_copy(k).wait_send()

    for k in range(1, 4):
        send(gs.at[1, mine], gs.at[1, mine], gs_sem.at[k - 1], gr_sem.at[q + 1],
             (dp, 4 * m + lax.rem(q + k, 4))).wait_send()

    @pl.when(edge)
    def _():
        for k in range(4):
            halo_copy(k).wait_send()

    for n in range(3):
        for k in range(1, NX):
            x_copy(n, k).wait_send()
    for yz in range(4):
        @pl.when(jnp.logical_not(y_is_self(yz)))
        def _():
            send(*early_refs(yz), y_target(yz)).wait_send()
            for n in range(3):
                send(*y_refs(n, yz), y_target(yz)).wait_send()

    @pl.when(active)
    def _():
        for k in range(1, NX):
            late_copy(k).wait_send()
        for s in range(BANDS):
            @pl.when(jnp.logical_not(z_is_self(s)))
            def _():
                z_copy(s).wait_send()

    for j in range(NSRC):
        arrived(rz.at[j], zr_sem.at[j])


def write_kernel(fg_in, rz_in, fg_out, wg_out, fg, rz, wg, in_sem, out_sem):
    parts = WRITES
    rows = PIX // parts
    first = pltpu.make_async_copy(rz_in, rz, in_sem.at[parts])
    first.start()
    copies = []
    for n in range(parts):
        at = pl.ds(n * rows, rows)
        copies.append((
            pltpu.make_async_copy(fg_in.at[at], fg.at[at], in_sem.at[n]),
            pltpu.make_async_copy(fg.at[at], fg_out.at[at], out_sem.at[n]),
        ))
        copies[-1][0].start()
    first.wait()
    total = rz[0].astype(F32)
    for j in range(1, NSRC):
        total = total + rz[j].astype(F32)
    wg[...] = total[:12] / IMAGES
    last = pltpu.make_async_copy(wg, wg_out, out_sem.at[parts])
    last.start()
    for load, store in copies:
        load.wait()
        store.start()
    for load, store in copies:
        store.wait()
    last.wait()


def on_device(features, labels, pixel_weight, conv_weight, conv_bias, class_weight):
    image = features.reshape(PIX, CIN)
    taps = conv_weight.transpose(1, 0, 2)
    hbm = pl.BlockSpec(memory_space=pltpu.HBM)
    dma = pltpu.SemaphoreType.DMA
    feature_grad, pieces = pl.pallas_call(
        step_kernel,
        out_shape=(
            jax.ShapeDtypeStruct((PIX, CIN), F32),
            jax.ShapeDtypeStruct((NSRC, 16, COUT), BF16),
        ),
        in_specs=[hbm] * 6,
        out_specs=(hbm, hbm),
        scratch_shapes=[
            pltpu.VMEM((PIX, CIN), BF16),
            pltpu.VMEM((9, CIN, COUT), BF16),
            pltpu.VMEM((ROWS, 1, COLS), jnp.int32),
            pltpu.VMEM((ROWS, 1, COLS), jnp.int32),
            pltpu.VMEM((1, COUT), F32),
            pltpu.VMEM((NCLS, COUT), BF16),
            pltpu.VMEM((4 * PIX, QUARTER), BF16),
            pltpu.VMEM((COUT, COUT), F32),
            pltpu.VMEM((2, PIX, COUT), F32),
            pltpu.VMEM((2, PIX, COUT), F32),
            pltpu.VMEM((3, 6 * PIX, COUT), BF16),
            pltpu.VMEM((2, NX, 192, COUT), BF16),
            pltpu.VMEM((2, NX - 1, 192, COUT), BF16),
            pltpu.VMEM((2, 192, COUT), BF16),
            pltpu.VMEM((2, NY, 48, COUT), BF16),
            pltpu.VMEM((NX, 64, COUT), BF16),
            pltpu.VMEM((NX - 1, 64, COUT), BF16),
            pltpu.VMEM((64, COUT), BF16),
            pltpu.VMEM((NY, 16, COUT), BF16),
            pltpu.VMEM((4, 128, COUT), BF16),
            pltpu.VMEM((NY, 128, COUT), BF16),
            pltpu.VMEM((NX, 32, COUT), BF16),
            pltpu.VMEM((NX - 1, 32, COUT), BF16),
            pltpu.VMEM((160, COUT), F32),
            pltpu.VMEM((BANDS, 16, COUT), BF16),
            pltpu.VMEM((PIX, CIN), F32),
            dma((8,)), dma((4,)), dma((2,)), dma((2,)), dma((4,)), dma((4,)), dma((3,)), dma((4,)), dma((6,)),
            dma((3, 3)), dma((3, 3)), dma((3, 4)), dma((3, NY)),
            dma((4,)), dma((NY,)), dma((3,)), dma((3,)), dma((BANDS,)), dma((NSRC,)),
        ],
        compiler_params=pltpu.CompilerParams(
            collective_id=0, has_side_effects=True, vmem_limit_bytes=VMEM_LIMIT),
        name="step",
    )(
        image, taps, labels.transpose(1, 0, 2), pixel_weight.transpose(1, 0, 2),
        conv_bias.reshape(1, COUT), class_weight.T,
    )
    feature_grad, weight_grad = pl.pallas_call(
        write_kernel,
        out_shape=(
            jax.ShapeDtypeStruct((PIX, CIN), F32),
            jax.ShapeDtypeStruct((12, COUT), F32),
        ),
        in_specs=[hbm] * 2,
        out_specs=(hbm, hbm),
        scratch_shapes=[
            pltpu.VMEM((PIX, CIN), F32),
            pltpu.VMEM((NSRC, 16, COUT), BF16),
            pltpu.VMEM((12, COUT), F32),
            dma((WRITES + 1,)), dma((WRITES + 1,)),
        ],
        compiler_params=pltpu.CompilerParams(vmem_limit_bytes=VMEM_LIMIT),
        name="write",
    )(feature_grad, pieces)
    return feature_grad.reshape(features.shape), weight_grad


def solution(mesh):
    placed = (
        P("dp", "space", None, None),
        P("dp", "space", None),
        P("dp", "space", None),
        P(),
        P(),
        P(),
    )
    return jax.shard_map(
        on_device,
        mesh=mesh,
        in_specs=placed,
        out_specs=(P("dp", "space", None, None), P(("dp", "space"), None)),
        check_vma=False,
    )
```

```python
import jax
import jax.numpy as jnp
from jax import lax
from jax.experimental import pallas as pl
from jax.experimental.pallas import tpu as pltpu
from jax.sharding import PartitionSpec as P

MESH = pl.DeviceIdType.MESH
F32 = jnp.float32
BF16 = jnp.bfloat16

ROWS, COLS, CIN, COUT, NCLS = 6, 32, 1024, 128, 3
SHIFT = 6
PIX = ROWS * COLS
QUARTER = CIN // 4
NX, NY = 4, 8
BANDS = 12
NSRC = 6
IMAGES = 64
WRITES = 8
VMEM_LIMIT = 60 * 1024 * 1024


def step_kernel(
    f_hbm, w_hbm, lab_hbm, pw_hbm, bias_hbm, cwt_hbm,
    fg_hbm, rz,
    fv, wv, lab_ref, pw_ref, bias_ref, cwt_ref,
    quarter, cwp, qs, rq, gs, con, rx, cy, ry, con1, rx1, cy1, ry1, early, early_in, late, late_in, pz, cz, fg,
    load_sem, out_sem, qs_sem, rq_sem, fs_sem, fr_sem, gs_sem, gh_sem, gr_sem,
    xs_sem, xr_sem, ys_sem, yr_sem, es_sem, er_sem, ls_sem, lr_sem, zs_sem, zr_sem,
):
    dp = lax.axis_index("dp")
    space = lax.axis_index("space")
    x = lax.rem(dp, NX)
    zh = lax.rem(lax.div(dp, NX), 2)
    y = lax.div(dp, 2 * NX)
    core = lax.rem(space, 2)
    zl = lax.div(space, 2)
    q = lax.rem(space, 4)
    m = lax.div(space, 4)
    odd = lax.rem(zl, 2)
    share = 2 * core + odd
    home = lax.div(y, 2)
    active = odd == lax.rem(home, 2)

    def dev(yy, hh, xx, ss):
        return ((yy * 2 + hh) * NX + xx, ss)

    def send(src, dst, send_sem, recv_sem, device):
        return pltpu.make_async_remote_copy(
            src, dst, send_sem, recv_sem, device_id=device, device_id_type=MESH)

    def arrived(dst, sem):
        pltpu.make_async_copy(dst, dst, sem).wait()

    loads = [pltpu.make_async_copy(f_hbm, fv, load_sem.at[0])]
    for n, a in enumerate((0, 2, 1)):
        loads.append(
            pltpu.make_async_copy(w_hbm.at[pl.ds(3 * a, 3)], wv.at[pl.ds(3 * a, 3)], load_sem.at[1 + n]))
    small = [
        pltpu.make_async_copy(src, dst, load_sem.at[4 + n])
        for n, (src, dst) in enumerate(
            ((cwt_hbm, cwt_ref), (bias_hbm, bias_ref), (lab_hbm, lab_ref), (pw_hbm, pw_ref)))
    ]
    for c in loads + small:
        c.start()

    barrier = pltpu.get_barrier_semaphore()

    def greet(device):
        pl.semaphore_signal(barrier, inc=1, device_id=device, device_id_type=MESH)

    for k in range(1, 4):
        greet((dp, 4 * m + lax.rem(q + k, 4)))
    for k in range(1, NX):
        greet(dev(y, zh, lax.rem(x + k, NX), space))

    @pl.when(m > 0)
    def _():
        greet((dp, 4 * m - 1))

    @pl.when(m < 2)
    def _():
        greet((dp, 4 * m + 4))

    for k in range(NY):
        @pl.when(jnp.logical_and(active, jnp.logical_or(share != home, y != k)))
        def _():
            greet(dev(k, zh, x, zl * 2 + lax.div(y, 4)))

    z_mine = jnp.logical_and(active, core == zh)
    slot = zh * 3 + m
    for j in range(NSRC):
        @pl.when(jnp.logical_not(jnp.logical_and(z_mine, slot == j)))
        def _():
            greet(dev(y, j // 3, x, (2 * (j % 3) + lax.rem(home, 2)) * 2 + zh))

    lower = jnp.logical_and(q == 0, m > 0)
    upper = jnp.logical_and(q == 3, m < 2)
    edge = jnp.logical_or(lower, upper)
    expected = (
        3 + jnp.where(edge, 4, 0) + 3 + (4 - jnp.where(share == home, 1, 0))
        + jnp.where(active, 12 - jnp.where(core == zh, 1, 0), 0)
    )

    column = lax.rem(lax.broadcasted_iota(jnp.int32, (PIX, COUT), 0), COLS)
    has_left = column >= SHIFT
    has_right = column < COLS - SHIFT

    def from_left(v):
        return jnp.where(has_left, pltpu.roll(v, SHIFT, 0), 0.0)

    def from_right(v):
        return jnp.where(has_right, pltpu.roll(v, PIX - SHIFT, 0), 0.0)

    def gather_taps(p):
        return p[:, COUT : 2 * COUT] + from_left(p[:, :COUT]) + from_right(p[:, 2 * COUT : 3 * COUT])

    def products(rows):
        w = jnp.concatenate([wv[3 * a + b] for a in rows for b in range(3)], axis=1)
        return jnp.dot(fv[...], w, preferred_element_type=F32)

    @pl.when(space == 0)
    def _():
        rq[0] = jnp.zeros((PIX, COUT), F32)
        gs[1, pl.ds(0, PIX)] = jnp.zeros((PIX, COUT), BF16)

    @pl.when(space == BANDS - 1)
    def _():
        rq[1] = jnp.zeros((PIX, COUT), F32)

    @pl.when(jnp.logical_and(m == 0, space != 0))
    def _():
        gs[1, pl.ds(0, PIX)] = jnp.zeros((PIX, COUT), BF16)

    @pl.when(m == 2)
    def _():
        gs[1, pl.ds(5 * PIX, PIX)] = jnp.zeros((PIX, COUT), BF16)

    cwp[...] = jnp.zeros((COUT, COUT), F32)
    pz[pl.ds(144, 16), :] = jnp.zeros((16, COUT), F32)

    loads[0].wait()
    loads[1].wait()
    loads[2].wait()
    both = products((0, 2))
    qs[0] = gather_taps(both[:, : 3 * COUT])
    qs[1] = gather_taps(both[:, 3 * COUT :])
    pl.semaphore_wait(barrier, expected)

    up = send(qs.at[0], rq.at[0], qs_sem.at[0], rq_sem.at[0], (dp, lax.rem(space + 1, BANDS)))
    down = send(qs.at[1], rq.at[1], qs_sem.at[1], rq_sem.at[1], (dp, lax.rem(space + BANDS - 1, BANDS)))

    @pl.when(space < BANDS - 1)
    def _():
        up.start()

    @pl.when(space > 0)
    def _():
        down.start()

    def band_of(k):
        return pl.ds(k * PIX, PIX)

    def quarter_copy(k):
        return send(
            fv.at[:, pl.ds((2 * (k % 2) + k // 2) * QUARTER, QUARTER)],
            quarter.at[pl.ds(pl.multiple_of(q * PIX, PIX), PIX)],
            fs_sem.at[k], fr_sem.at[q], (dp, 4 * m + k))

    for k in range(4):
        @pl.when(q != k)
        def _():
            quarter_copy(k).start()

        @pl.when(q == k)
        def _():
            pltpu.make_async_copy(
                fv.at[:, pl.ds((2 * (k % 2) + k // 2) * QUARTER, QUARTER)],
                quarter.at[band_of(k)], fr_sem.at[q]).start()

    loads[3].wait()
    for c in small:
        c.wait()
    cwp[pl.ds(0, NCLS), :] = cwt_ref[...].astype(F32)
    local = gather_taps(products((1,))) + bias_ref[...]

    eye = (
        lax.broadcasted_iota(jnp.int32, (COLS, COLS), 0)
        == lax.broadcasted_iota(jnp.int32, (COLS, COLS), 1)
    )

    def per_pixel(ref):
        return jnp.concatenate(
            [
                jnp.sum(
                    jnp.where(eye, jnp.broadcast_to(ref[r].astype(F32), (COLS, COLS)), 0.0),
                    axis=1, keepdims=True,
                )
                for r in range(ROWS)
            ],
            axis=0,
        )

    label = per_pixel(lab_ref)
    weight = per_pixel(pw_ref)

    @pl.when(space > 0)
    def _():
        up.wait_recv()

    @pl.when(space < BANDS - 1)
    def _():
        down.wait_recv()

    preact = local + rq[0] + rq[1]
    sig = jax.nn.sigmoid(preact)
    hidden = (preact * sig).astype(BF16)
    proj = cwp[...]
    logits = lax.dot_general(
        hidden, proj.astype(BF16), (((1,), (1,)), ((), ())), preferred_element_type=F32)
    lane = lax.broadcasted_iota(jnp.int32, (PIX, COUT), 1)
    real = lane < NCLS
    expo = jnp.where(real, jnp.exp(logits), 0.0)
    chances = expo / jnp.sum(expo, axis=1, keepdims=True)
    onehot = jnp.where(lane.astype(F32) == label, 1.0, 0.0)
    grad_logits = jnp.where(real, weight * (chances - onehot), 0.0)
    hidden_grad = lax.dot_general(
        grad_logits, proj, (((1,), (0,)), ((), ())),
        precision=lax.Precision.HIGHEST, preferred_element_type=F32)
    grad = hidden_grad * sig * (1.0 + preact * (1.0 - sig))

    def window(w):
        return pl.ds(pl.multiple_of(w * PIX, PIX), PIX)

    mine = window(q + 1)
    gs[1, mine] = grad.astype(BF16)
    partner = (dp, zl * 2 + 1 - core)

    def across(k):
        to = lax.rem(q + 2, 4) if k == 0 else 2 * lax.div(q, 2) + 1 - core
        return send(gs.at[1, mine], gs.at[1, mine], gs_sem.at[k], gr_sem.at[q + 1], (dp, 4 * m + to))

    def hand_on(k, w):
        return send(gs.at[1, window(w)], gs.at[1, window(w)], gs_sem.at[2 + k], gr_sem.at[w], partner)

    across(0).start()
    across(1).start()

    def halo_copy(k):
        return send(
            gs.at[1, mine], gs.at[1, window(jnp.where(q == 0, 5, 0))],
            gh_sem.at[k], gr_sem.at[jnp.where(q == 0, 5, 0)],
            (dp, lax.rem(4 * (m + jnp.where(q == 0, 2, 1)), BANDS) + 2 * k + core))

    @pl.when(edge)
    def _():
        for k in range(2):
            halo_copy(k).start()

    def spread(w):
        g = gs[1, window(w)].astype(F32)
        gs[0, window(w)] = from_right(g).astype(BF16)
        gs[2, window(w)] = from_left(g).astype(BF16)

    spread(q + 1)
    for k in range(4):
        arrived(quarter.at[band_of(k)], fr_sem.at[k])
    columns = quarter[...].T
    opposite = 1 + lax.rem(q + 2, 4)
    arrived(gs.at[1, window(opposite)], gr_sem.at[opposite])
    hand_on(0, opposite).start()
    spread(opposite)
    beside = 1 + 2 * lax.div(q, 2) + 1 - core
    arrived(gs.at[1, window(beside)], gr_sem.at[beside])
    spread(beside)
    last = 1 + lax.rem(beside + 1, 4)
    arrived(gs.at[1, window(last)], gr_sem.at[last])
    spread(last)

    def group(n, wide, narrow):
        return narrow if n == 0 else wide.at[n - 1]

    def group_rows(n):
        return 16 if n == 0 else 48

    def x_copy(n, k):
        to = lax.rem(x + k, NX)
        return send(
            group(n, con, con1).at[to], group(n, rx, rx1).at[k - 1],
            xs_sem.at[n, k - 1], xr_sem.at[n, k - 1], dev(y, zh, to, space))

    def y_target(yz):
        return dev(2 * share + yz // 2, zh, x, zl * 2 + yz % 2)

    def y_is_self(yz):
        return jnp.logical_and(y == 2 * share + yz // 2, core == yz % 2)

    def y_send(src, dst, send_sem, recv_sem, yz):
        itself = y_is_self(yz)

        @pl.when(itself)
        def _():
            pltpu.make_async_copy(src, dst, recv_sem).start()

        @pl.when(jnp.logical_not(itself))
        def _():
            send(src, dst, send_sem, recv_sem, y_target(yz)).start()

    def early_refs(yz):
        return early.at[yz], early_in.at[y], es_sem.at[yz], er_sem.at[y]

    def contribute(a):
        rhs = jnp.concatenate(
            [gs[b, pl.ds((2 - a) * PIX, 4 * PIX)] for b in range(3)], axis=1)
        total = jnp.dot(columns, rhs, preferred_element_type=F32).astype(BF16)
        for c in range(QUARTER // 16):
            yz, xd = divmod(c, NX)
            for b in range(3):
                piece = total[c * 16 : (c + 1) * 16, b * COUT : (b + 1) * COUT]
                if a != 1:
                    con[a // 2, xd, pl.ds((yz * 3 + b) * 16, 16), :] = piece
                elif b == 0:
                    con1[xd, pl.ds(yz * 16, 16), :] = piece
                else:
                    early[yz, pl.ds((xd * 2 + b - 1) * 16, 16), :] = piece
        for k in (2, 1, 3):
            x_copy((1, 0, 2)[a], k).start()
        if a == 1:
            for yz in range(4):
                y_send(*early_refs(yz), yz)

    contribute(1)

    @pl.when(m < 2)
    def _():
        arrived(gs.at[1, window(5)], gr_sem.at[5])

    @pl.when(jnp.logical_and(m < 2, core == 0))
    def _():
        hand_on(1, 5).start()

    spread(5)
    contribute(0)

    @pl.when(m > 0)
    def _():
        arrived(gs.at[1, window(0)], gr_sem.at[0])

    @pl.when(jnp.logical_and(m > 0, core == 1))
    def _():
        hand_on(1, 0).start()

    spread(0)
    contribute(2)

    around = jnp.concatenate(
        [gs[b, window(q + 2 - a)] for a in range(3) for b in range(3)], axis=1)
    outs = []
    for n in range(4):
        width = CIN // 4
        wn = jnp.concatenate([wv[t, pl.ds(n * width, width)] for t in range(9)], axis=1)
        fg[:, pl.ds(n * width, width)] = lax.dot_general(
            around, wn, (((1,), (1,)), ((), ())), preferred_element_type=F32)
        outs.append(
            pltpu.make_async_copy(
                fg.at[:, pl.ds(n * width, width)], fg_hbm.at[:, pl.ds(n * width, width)],
                out_sem.at[n]))
        outs[-1].start()

    def y_refs(n, yz):
        rows = group_rows(n)
        return (
            group(n, cy, cy1).at[pl.ds(yz * rows, rows)], group(n, ry, ry1).at[y],
            ys_sem.at[n, yz], yr_sem.at[n, y])

    for n in range(3):
        for k in (2, 1, 3):
            x_copy(n, k).wait_recv()
        total = group(n, con, con1)[x].astype(F32)
        for k in range(3):
            total = total + group(n, rx, rx1)[k].astype(F32)
        group(n, cy, cy1)[...] = total.astype(BF16)
        for yz in range(4):
            y_send(*y_refs(n, yz), yz)

    def late_copy(k):
        to = lax.rem(x + k, NX)
        return send(
            late.at[to], late_in.at[k - 1], ls_sem.at[k - 1], lr_sem.at[k - 1],
            dev(y, zh, to, space))

    def z_copy(s):
        return send(cz.at[s], rz.at[slot], zs_sem.at[s], zr_sem.at[slot], dev(y, core, x, s))

    def z_is_self(s):
        return jnp.logical_and(core == zh, space == s)

    @pl.when(active)
    def _():
        total = None
        for k in range(NY):
            arrived(early_in.at[k], er_sem.at[k])
            part = early_in[k].astype(F32)
            total = part if total is None else total + part
        for to in range(NX):
            late[to] = total[to * 32 : (to + 1) * 32].astype(BF16)
        for k in (2, 1, 3):
            late_copy(k).start()
        for n in range(3):
            total = None
            for k in range(NY):
                arrived(group(n, ry, ry1).at[k], yr_sem.at[n, k])
                part = group(n, ry, ry1)[k].astype(F32)
                total = part if total is None else total + part
            for b, tap in enumerate(((3,), (0, 1, 2), (6, 7, 8))[n]):
                pz[pl.ds(tap, 16, stride=9), :] = total[b * 16 : (b + 1) * 16]
        total = late[x].astype(F32)
        for k in (2, 1, 3):
            late_copy(k).wait_recv()
            total = total + late_in[k - 1].astype(F32)
        for b in range(2):
            pz[pl.ds(4 + b, 16, stride=9), :] = total[b * 16 : (b + 1) * 16]
        for s in range(BANDS):
            cz[s] = pz[pl.ds(12 * s, 16), :].astype(BF16)
        for s in range(BANDS):
            @pl.when(z_is_self(s))
            def _():
                pltpu.make_async_copy(cz.at[s], rz.at[slot], zr_sem.at[slot]).start()

            @pl.when(jnp.logical_not(z_is_self(s)))
            def _():
                z_copy(s).start()

    for c in outs:
        c.wait()

    @pl.when(space < BANDS - 1)
    def _():
        up.wait_send()

    @pl.when(space > 0)
    def _():
        down.wait_send()

    for k in range(4):
        @pl.when(q != k)
        def _():
            quarter_copy(k).wait_send()

    across(0).wait_send()
    across(1).wait_send()
    hand_on(0, opposite).wait_send()

    @pl.when(jnp.logical_and(m < 2, core == 0))
    def _():
        hand_on(1, 5).wait_send()

    @pl.when(jnp.logical_and(m > 0, core == 1))
    def _():
        hand_on(1, 0).wait_send()

    @pl.when(edge)
    def _():
        for k in range(2):
            halo_copy(k).wait_send()

    for n in range(3):
        for k in range(1, NX):
            x_copy(n, k).wait_send()
    for yz in range(4):
        @pl.when(jnp.logical_not(y_is_self(yz)))
        def _():
            send(*early_refs(yz), y_target(yz)).wait_send()
            for n in range(3):
                send(*y_refs(n, yz), y_target(yz)).wait_send()

    @pl.when(active)
    def _():
        for k in range(1, NX):
            late_copy(k).wait_send()
        for s in range(BANDS):
            @pl.when(jnp.logical_not(z_is_self(s)))
            def _():
                z_copy(s).wait_send()

    for j in range(NSRC):
        arrived(rz.at[j], zr_sem.at[j])


def write_kernel(fg_in, rz_in, fg_out, wg_out, fg, rz, wg, in_sem, out_sem):
    parts = WRITES
    rows = PIX // parts
    first = pltpu.make_async_copy(rz_in, rz, in_sem.at[parts])
    first.start()
    copies = []
    for n in range(parts):
        at = pl.ds(n * rows, rows)
        copies.append((
            pltpu.make_async_copy(fg_in.at[at], fg.at[at], in_sem.at[n]),
            pltpu.make_async_copy(fg.at[at], fg_out.at[at], out_sem.at[n]),
        ))
        copies[-1][0].start()
    first.wait()
    total = rz[0].astype(F32)
    for j in range(1, NSRC):
        total = total + rz[j].astype(F32)
    wg[...] = total[:12] / IMAGES
    last = pltpu.make_async_copy(wg, wg_out, out_sem.at[parts])
    last.start()
    for load, store in copies:
        load.wait()
        store.start()
    for load, store in copies:
        store.wait()
    last.wait()


def on_device(features, labels, pixel_weight, conv_weight, conv_bias, class_weight):
    image = features.reshape(PIX, CIN)
    taps = conv_weight.transpose(1, 0, 2)
    hbm = pl.BlockSpec(memory_space=pltpu.HBM)
    dma = pltpu.SemaphoreType.DMA
    feature_grad, pieces = pl.pallas_call(
        step_kernel,
        out_shape=(
            jax.ShapeDtypeStruct((PIX, CIN), F32),
            jax.ShapeDtypeStruct((NSRC, 16, COUT), BF16),
        ),
        in_specs=[hbm] * 6,
        out_specs=(hbm, hbm),
        scratch_shapes=[
            pltpu.VMEM((PIX, CIN), BF16),
            pltpu.VMEM((9, CIN, COUT), BF16),
            pltpu.VMEM((ROWS, 1, COLS), jnp.int32),
            pltpu.VMEM((ROWS, 1, COLS), jnp.int32),
            pltpu.VMEM((1, COUT), F32),
            pltpu.VMEM((NCLS, COUT), BF16),
            pltpu.VMEM((4 * PIX, QUARTER), BF16),
            pltpu.VMEM((COUT, COUT), F32),
            pltpu.VMEM((2, PIX, COUT), F32),
            pltpu.VMEM((2, PIX, COUT), F32),
            pltpu.VMEM((3, 6 * PIX, COUT), BF16),
            pltpu.VMEM((2, NX, 192, COUT), BF16),
            pltpu.VMEM((2, NX - 1, 192, COUT), BF16),
            pltpu.VMEM((2, 192, COUT), BF16),
            pltpu.VMEM((2, NY, 48, COUT), BF16),
            pltpu.VMEM((NX, 64, COUT), BF16),
            pltpu.VMEM((NX - 1, 64, COUT), BF16),
            pltpu.VMEM((64, COUT), BF16),
            pltpu.VMEM((NY, 16, COUT), BF16),
            pltpu.VMEM((4, 128, COUT), BF16),
            pltpu.VMEM((NY, 128, COUT), BF16),
            pltpu.VMEM((NX, 32, COUT), BF16),
            pltpu.VMEM((NX - 1, 32, COUT), BF16),
            pltpu.VMEM((160, COUT), F32),
            pltpu.VMEM((BANDS, 16, COUT), BF16),
            pltpu.VMEM((PIX, CIN), F32),
            dma((8,)), dma((4,)), dma((2,)), dma((2,)), dma((4,)), dma((4,)), dma((4,)), dma((2,)), dma((6,)),
            dma((3, 3)), dma((3, 3)), dma((3, 4)), dma((3, NY)),
            dma((4,)), dma((NY,)), dma((3,)), dma((3,)), dma((BANDS,)), dma((NSRC,)),
        ],
        compiler_params=pltpu.CompilerParams(
            collective_id=0, has_side_effects=True, vmem_limit_bytes=VMEM_LIMIT),
        name="step",
    )(
        image, taps, labels.transpose(1, 0, 2), pixel_weight.transpose(1, 0, 2),
        conv_bias.reshape(1, COUT), class_weight.T,
    )
    feature_grad, weight_grad = pl.pallas_call(
        write_kernel,
        out_shape=(
            jax.ShapeDtypeStruct((PIX, CIN), F32),
            jax.ShapeDtypeStruct((12, COUT), F32),
        ),
        in_specs=[hbm] * 2,
        out_specs=(hbm, hbm),
        scratch_shapes=[
            pltpu.VMEM((PIX, CIN), F32),
            pltpu.VMEM((NSRC, 16, COUT), BF16),
            pltpu.VMEM((12, COUT), F32),
            dma((WRITES + 1,)), dma((WRITES + 1,)),
        ],
        compiler_params=pltpu.CompilerParams(vmem_limit_bytes=VMEM_LIMIT),
        name="write",
    )(feature_grad, pieces)
    return feature_grad.reshape(features.shape), weight_grad


def solution(mesh):
    placed = (
        P("dp", "space", None, None),
        P("dp", "space", None),
        P("dp", "space", None),
        P(),
        P(),
        P(),
    )
    return jax.shard_map(
        on_device,
        mesh=mesh,
        in_specs=placed,
        out_specs=(P("dp", "space", None, None), P(("dp", "space"), None)),
        check_vma=False,
    )
```

```python
import jax
import jax.numpy as jnp
from jax import lax
from jax.experimental import pallas as pl
from jax.experimental.pallas import tpu as pltpu
from jax.sharding import PartitionSpec as P

MESH = pl.DeviceIdType.MESH
F32 = jnp.float32
BF16 = jnp.bfloat16

ROWS, COLS, CIN, COUT, NCLS = 6, 32, 1024, 128, 3
SHIFT = 6
PIX = ROWS * COLS
QUARTER = CIN // 4
NX, NY = 4, 8
BANDS = 12
NSRC = 6
IMAGES = 64
WRITES = 3
VMEM_LIMIT = 60 * 1024 * 1024


def step_kernel(
    f_hbm, w_hbm, lab_hbm, pw_hbm, bias_hbm, cwt_hbm,
    fg_hbm, rz,
    fv, wv, lab_ref, pw_ref, bias_ref, cwt_ref,
    quarter, cwp, qs, rq, gs, con, rx, cy, ry, con1, rx1, cy1, ry1, early, early_in, late, late_in, pz, cz, fg,
    load_sem, out_sem, qs_sem, rq_sem, fs_sem, fr_sem, gs_sem, gh_sem, gr_sem,
    xs_sem, xr_sem, ys_sem, yr_sem, es_sem, er_sem, ls_sem, lr_sem, zs_sem, zr_sem,
):
    dp = lax.axis_index("dp")
    space = lax.axis_index("space")
    x = lax.rem(dp, NX)
    zh = lax.rem(lax.div(dp, NX), 2)
    y = lax.div(dp, 2 * NX)
    core = lax.rem(space, 2)
    zl = lax.div(space, 2)
    q = lax.rem(space, 4)
    m = lax.div(space, 4)
    odd = lax.rem(zl, 2)
    share = 2 * core + odd
    home = lax.div(y, 2)
    active = odd == lax.rem(home, 2)

    def dev(yy, hh, xx, ss):
        return ((yy * 2 + hh) * NX + xx, ss)

    def send(src, dst, send_sem, recv_sem, device):
        return pltpu.make_async_remote_copy(
            src, dst, send_sem, recv_sem, device_id=device, device_id_type=MESH)

    def arrived(dst, sem):
        pltpu.make_async_copy(dst, dst, sem).wait()

    loads = [pltpu.make_async_copy(f_hbm, fv, load_sem.at[0])]
    for n, a in enumerate((0, 2, 1)):
        loads.append(
            pltpu.make_async_copy(w_hbm.at[pl.ds(3 * a, 3)], wv.at[pl.ds(3 * a, 3)], load_sem.at[1 + n]))
    small = [
        pltpu.make_async_copy(src, dst, load_sem.at[4 + n])
        for n, (src, dst) in enumerate(
            ((cwt_hbm, cwt_ref), (bias_hbm, bias_ref), (lab_hbm, lab_ref), (pw_hbm, pw_ref)))
    ]
    for c in loads + small:
        c.start()

    barrier = pltpu.get_barrier_semaphore()

    def greet(device):
        pl.semaphore_signal(barrier, inc=1, device_id=device, device_id_type=MESH)

    for k in range(1, 4):
        greet((dp, 4 * m + lax.rem(q + k, 4)))
    for k in range(1, NX):
        greet(dev(y, zh, lax.rem(x + k, NX), space))

    @pl.when(m > 0)
    def _():
        greet((dp, 4 * m - 1))

    @pl.when(m < 2)
    def _():
        greet((dp, 4 * m + 4))

    for k in range(NY):
        @pl.when(jnp.logical_and(active, jnp.logical_or(share != home, y != k)))
        def _():
            greet(dev(k, zh, x, zl * 2 + lax.div(y, 4)))

    z_mine = jnp.logical_and(active, core == zh)
    slot = zh * 3 + m
    for j in range(NSRC):
        @pl.when(jnp.logical_not(jnp.logical_and(z_mine, slot == j)))
        def _():
            greet(dev(y, j // 3, x, (2 * (j % 3) + lax.rem(home, 2)) * 2 + zh))

    lower = jnp.logical_and(q == 0, m > 0)
    upper = jnp.logical_and(q == 3, m < 2)
    edge = jnp.logical_or(lower, upper)
    expected = (
        3 + jnp.where(edge, 4, 0) + 3 + (4 - jnp.where(share == home, 1, 0))
        + jnp.where(active, 12 - jnp.where(core == zh, 1, 0), 0)
    )

    column = lax.rem(lax.broadcasted_iota(jnp.int32, (PIX, COUT), 0), COLS)
    has_left = column >= SHIFT
    has_right = column < COLS - SHIFT

    def from_left(v):
        return jnp.where(has_left, pltpu.roll(v, SHIFT, 0), 0.0)

    def from_right(v):
        return jnp.where(has_right, pltpu.roll(v, PIX - SHIFT, 0), 0.0)

    def gather_taps(p):
        return p[:, COUT : 2 * COUT] + from_left(p[:, :COUT]) + from_right(p[:, 2 * COUT : 3 * COUT])

    def products(rows):
        w = jnp.concatenate([wv[3 * a + b] for a in rows for b in range(3)], axis=1)
        return jnp.dot(fv[...], w, preferred_element_type=F32)

    @pl.when(space == 0)
    def _():
        rq[0] = jnp.zeros((PIX, COUT), F32)
        gs[1, pl.ds(0, PIX)] = jnp.zeros((PIX, COUT), BF16)

    @pl.when(space == BANDS - 1)
    def _():
        rq[1] = jnp.zeros((PIX, COUT), F32)

    @pl.when(jnp.logical_and(m == 0, space != 0))
    def _():
        gs[1, pl.ds(0, PIX)] = jnp.zeros((PIX, COUT), BF16)

    @pl.when(m == 2)
    def _():
        gs[1, pl.ds(5 * PIX, PIX)] = jnp.zeros((PIX, COUT), BF16)

    cwp[...] = jnp.zeros((COUT, COUT), F32)
    pz[pl.ds(144, 16), :] = jnp.zeros((16, COUT), F32)

    loads[0].wait()
    loads[1].wait()
    loads[2].wait()
    both = products((0, 2))
    qs[0] = gather_taps(both[:, : 3 * COUT])
    qs[1] = gather_taps(both[:, 3 * COUT :])
    pl.semaphore_wait(barrier, expected)

    up = send(qs.at[0], rq.at[0], qs_sem.at[0], rq_sem.at[0], (dp, lax.rem(space + 1, BANDS)))
    down = send(qs.at[1], rq.at[1], qs_sem.at[1], rq_sem.at[1], (dp, lax.rem(space + BANDS - 1, BANDS)))

    @pl.when(space < BANDS - 1)
    def _():
        up.start()

    @pl.when(space > 0)
    def _():
        down.start()

    def band_of(k):
        return pl.ds(k * PIX, PIX)

    def quarter_copy(k):
        return send(
            fv.at[:, pl.ds((2 * (k % 2) + k // 2) * QUARTER, QUARTER)],
            quarter.at[pl.ds(pl.multiple_of(q * PIX, PIX), PIX)],
            fs_sem.at[k], fr_sem.at[q], (dp, 4 * m + k))

    for k in range(4):
        @pl.when(q != k)
        def _():
            quarter_copy(k).start()

        @pl.when(q == k)
        def _():
            pltpu.make_async_copy(
                fv.at[:, pl.ds((2 * (k % 2) + k // 2) * QUARTER, QUARTER)],
                quarter.at[band_of(k)], fr_sem.at[q]).start()

    loads[3].wait()
    for c in small:
        c.wait()
    cwp[pl.ds(0, NCLS), :] = cwt_ref[...].astype(F32)
    local = gather_taps(products((1,))) + bias_ref[...]

    eye = (
        lax.broadcasted_iota(jnp.int32, (COLS, COLS), 0)
        == lax.broadcasted_iota(jnp.int32, (COLS, COLS), 1)
    )

    def per_pixel(ref):
        return jnp.concatenate(
            [
                jnp.sum(
                    jnp.where(eye, jnp.broadcast_to(ref[r].astype(F32), (COLS, COLS)), 0.0),
                    axis=1, keepdims=True,
                )
                for r in range(ROWS)
            ],
            axis=0,
        )

    label = per_pixel(lab_ref)
    weight = per_pixel(pw_ref)

    @pl.when(space > 0)
    def _():
        up.wait_recv()

    @pl.when(space < BANDS - 1)
    def _():
        down.wait_recv()

    preact = local + rq[0] + rq[1]
    sig = jax.nn.sigmoid(preact)
    hidden = (preact * sig).astype(BF16)
    proj = cwp[...]
    logits = lax.dot_general(
        hidden, proj.astype(BF16), (((1,), (1,)), ((), ())), preferred_element_type=F32)
    lane = lax.broadcasted_iota(jnp.int32, (PIX, COUT), 1)
    real = lane < NCLS
    expo = jnp.where(real, jnp.exp(logits), 0.0)
    chances = expo / jnp.sum(expo, axis=1, keepdims=True)
    onehot = jnp.where(lane.astype(F32) == label, 1.0, 0.0)
    grad_logits = jnp.where(real, weight * (chances - onehot), 0.0)
    hidden_grad = lax.dot_general(
        grad_logits, proj, (((1,), (0,)), ((), ())),
        precision=lax.Precision.HIGHEST, preferred_element_type=F32)
    grad = hidden_grad * sig * (1.0 + preact * (1.0 - sig))

    def window(w):
        return pl.ds(pl.multiple_of(w * PIX, PIX), PIX)

    mine = window(q + 1)
    gs[1, mine] = grad.astype(BF16)
    partner = (dp, zl * 2 + 1 - core)

    def across(k):
        to = lax.rem(q + 2, 4) if k == 0 else 2 * lax.div(q, 2) + 1 - core
        return send(gs.at[1, mine], gs.at[1, mine], gs_sem.at[k], gr_sem.at[q + 1], (dp, 4 * m + to))

    def hand_on(k, w):
        return send(gs.at[1, window(w)], gs.at[1, window(w)], gs_sem.at[2 + k], gr_sem.at[w], partner)

    across(0).start()
    across(1).start()

    def halo_copy(k):
        return send(
            gs.at[1, mine], gs.at[1, window(jnp.where(q == 0, 5, 0))],
            gh_sem.at[k], gr_sem.at[jnp.where(q == 0, 5, 0)],
            (dp, lax.rem(4 * (m + jnp.where(q == 0, 2, 1)), BANDS) + 2 * k + core))

    @pl.when(edge)
    def _():
        for k in range(2):
            halo_copy(k).start()

    def spread(w):
        g = gs[1, window(w)].astype(F32)
        gs[0, window(w)] = from_right(g).astype(BF16)
        gs[2, window(w)] = from_left(g).astype(BF16)

    spread(q + 1)
    for k in range(4):
        arrived(quarter.at[band_of(k)], fr_sem.at[k])
    columns = quarter[...].T
    opposite = 1 + lax.rem(q + 2, 4)
    arrived(gs.at[1, window(opposite)], gr_sem.at[opposite])
    hand_on(0, opposite).start()
    spread(opposite)
    beside = 1 + 2 * lax.div(q, 2) + 1 - core
    arrived(gs.at[1, window(beside)], gr_sem.at[beside])
    spread(beside)
    last = 1 + lax.rem(beside + 1, 4)
    arrived(gs.at[1, window(last)], gr_sem.at[last])
    spread(last)

    def group(n, wide, narrow):
        return narrow if n == 0 else wide.at[n - 1]

    def group_rows(n):
        return 16 if n == 0 else 48

    def x_copy(n, k):
        to = lax.rem(x + k, NX)
        return send(
            group(n, con, con1).at[to], group(n, rx, rx1).at[k - 1],
            xs_sem.at[n, k - 1], xr_sem.at[n, k - 1], dev(y, zh, to, space))

    def y_target(yz):
        return dev(2 * share + yz // 2, zh, x, zl * 2 + yz % 2)

    def y_is_self(yz):
        return jnp.logical_and(y == 2 * share + yz // 2, core == yz % 2)

    def y_send(src, dst, send_sem, recv_sem, yz):
        itself = y_is_self(yz)

        @pl.when(itself)
        def _():
            pltpu.make_async_copy(src, dst, recv_sem).start()

        @pl.when(jnp.logical_not(itself))
        def _():
            send(src, dst, send_sem, recv_sem, y_target(yz)).start()

    def early_refs(yz):
        return early.at[yz], early_in.at[y], es_sem.at[yz], er_sem.at[y]

    def contribute(a):
        rhs = jnp.concatenate(
            [gs[b, pl.ds((2 - a) * PIX, 4 * PIX)] for b in range(3)], axis=1)
        total = jnp.dot(columns, rhs, preferred_element_type=F32).astype(BF16)
        for c in range(QUARTER // 16):
            yz, xd = divmod(c, NX)
            for b in range(3):
                piece = total[c * 16 : (c + 1) * 16, b * COUT : (b + 1) * COUT]
                if a != 1:
                    con[a // 2, xd, pl.ds((yz * 3 + b) * 16, 16), :] = piece
                elif b == 0:
                    con1[xd, pl.ds(yz * 16, 16), :] = piece
                else:
                    early[yz, pl.ds((xd * 2 + b - 1) * 16, 16), :] = piece
        if a == 1:
            for yz in range(4):
                y_send(*early_refs(yz), yz)
        for k in (2, 1, 3):
            x_copy((1, 0, 2)[a], k).start()

    contribute(1)

    @pl.when(m < 2)
    def _():
        arrived(gs.at[1, window(5)], gr_sem.at[5])

    @pl.when(jnp.logical_and(m < 2, core == 0))
    def _():
        hand_on(1, 5).start()

    spread(5)
    contribute(0)

    @pl.when(m > 0)
    def _():
        arrived(gs.at[1, window(0)], gr_sem.at[0])

    @pl.when(jnp.logical_and(m > 0, core == 1))
    def _():
        hand_on(1, 0).start()

    spread(0)
    contribute(2)

    around = jnp.concatenate(
        [gs[b, window(q + 2 - a)] for a in range(3) for b in range(3)], axis=1)
    outs = []
    for n in range(4):
        width = CIN // 4
        wn = jnp.concatenate([wv[t, pl.ds(n * width, width)] for t in range(9)], axis=1)
        fg[:, pl.ds(n * width, width)] = lax.dot_general(
            around, wn, (((1,), (1,)), ((), ())), preferred_element_type=F32)
        outs.append(
            pltpu.make_async_copy(
                fg.at[:, pl.ds(n * width, width)], fg_hbm.at[:, pl.ds(n * width, width)],
                out_sem.at[n]))
        outs[-1].start()

    def y_refs(n, yz):
        rows = group_rows(n)
        return (
            group(n, cy, cy1).at[pl.ds(yz * rows, rows)], group(n, ry, ry1).at[y],
            ys_sem.at[n, yz], yr_sem.at[n, y])

    for n in range(3):
        for k in (2, 1, 3):
            x_copy(n, k).wait_recv()
        total = group(n, con, con1)[x].astype(F32)
        for k in range(3):
            total = total + group(n, rx, rx1)[k].astype(F32)
        group(n, cy, cy1)[...] = total.astype(BF16)
        for yz in range(4):
            y_send(*y_refs(n, yz), yz)

    def late_copy(k):
        to = lax.rem(x + k, NX)
        return send(
            late.at[to], late_in.at[k - 1], ls_sem.at[k - 1], lr_sem.at[k - 1],
            dev(y, zh, to, space))

    def z_copy(s):
        return send(cz.at[s], rz.at[slot], zs_sem.at[s], zr_sem.at[slot], dev(y, core, x, s))

    def z_is_self(s):
        return jnp.logical_and(core == zh, space == s)

    @pl.when(active)
    def _():
        total = None
        for k in range(NY):
            arrived(early_in.at[k], er_sem.at[k])
            part = early_in[k].astype(F32)
            total = part if total is None else total + part
        for to in range(NX):
            late[to] = total[to * 32 : (to + 1) * 32].astype(BF16)
        for k in (2, 1, 3):
            late_copy(k).start()
        for n in range(3):
            total = None
            for k in range(NY):
                arrived(group(n, ry, ry1).at[k], yr_sem.at[n, k])
                part = group(n, ry, ry1)[k].astype(F32)
                total = part if total is None else total + part
            for b, tap in enumerate(((3,), (0, 1, 2), (6, 7, 8))[n]):
                pz[pl.ds(tap, 16, stride=9), :] = total[b * 16 : (b + 1) * 16]
        total = late[x].astype(F32)
        for k in (2, 1, 3):
            late_copy(k).wait_recv()
            total = total + late_in[k - 1].astype(F32)
        for b in range(2):
            pz[pl.ds(4 + b, 16, stride=9), :] = total[b * 16 : (b + 1) * 16]
        for s in range(BANDS):
            cz[s] = pz[pl.ds(12 * s, 16), :].astype(BF16)
        for s in range(BANDS):
            @pl.when(z_is_self(s))
            def _():
                pltpu.make_async_copy(cz.at[s], rz.at[slot], zr_sem.at[slot]).start()

            @pl.when(jnp.logical_not(z_is_self(s)))
            def _():
                z_copy(s).start()

    for c in outs:
        c.wait()

    @pl.when(space < BANDS - 1)
    def _():
        up.wait_send()

    @pl.when(space > 0)
    def _():
        down.wait_send()

    for k in range(4):
        @pl.when(q != k)
        def _():
            quarter_copy(k).wait_send()

    across(0).wait_send()
    across(1).wait_send()
    hand_on(0, opposite).wait_send()

    @pl.when(jnp.logical_and(m < 2, core == 0))
    def _():
        hand_on(1, 5).wait_send()

    @pl.when(jnp.logical_and(m > 0, core == 1))
    def _():
        hand_on(1, 0).wait_send()

    @pl.when(edge)
    def _():
        for k in range(2):
            halo_copy(k).wait_send()

    for n in range(3):
        for k in range(1, NX):
            x_copy(n, k).wait_send()
    for yz in range(4):
        @pl.when(jnp.logical_not(y_is_self(yz)))
        def _():
            send(*early_refs(yz), y_target(yz)).wait_send()
            for n in range(3):
                send(*y_refs(n, yz), y_target(yz)).wait_send()

    @pl.when(active)
    def _():
        for k in range(1, NX):
            late_copy(k).wait_send()
        for s in range(BANDS):
            @pl.when(jnp.logical_not(z_is_self(s)))
            def _():
                z_copy(s).wait_send()

    for j in range(NSRC):
        arrived(rz.at[j], zr_sem.at[j])


def write_kernel(fg_in, rz_in, fg_out, wg_out, fg, rz, wg, in_sem, out_sem):
    parts = WRITES
    rows = PIX // parts
    first = pltpu.make_async_copy(rz_in, rz, in_sem.at[parts])
    first.start()
    copies = []
    for n in range(parts):
        at = pl.ds(n * rows, rows)
        copies.append((
            pltpu.make_async_copy(fg_in.at[at], fg.at[at], in_sem.at[n]),
            pltpu.make_async_copy(fg.at[at], fg_out.at[at], out_sem.at[n]),
        ))
        copies[-1][0].start()
    first.wait()
    total = rz[0].astype(F32)
    for j in range(1, NSRC):
        total = total + rz[j].astype(F32)
    wg[...] = total[:12] / IMAGES
    last = pltpu.make_async_copy(wg, wg_out, out_sem.at[parts])
    last.start()
    for load, store in copies:
        load.wait()
        store.start()
    for load, store in copies:
        store.wait()
    last.wait()


def on_device(features, labels, pixel_weight, conv_weight, conv_bias, class_weight):
    image = features.reshape(PIX, CIN)
    taps = conv_weight.transpose(1, 0, 2)
    hbm = pl.BlockSpec(memory_space=pltpu.HBM)
    dma = pltpu.SemaphoreType.DMA
    feature_grad, pieces = pl.pallas_call(
        step_kernel,
        out_shape=(
            jax.ShapeDtypeStruct((PIX, CIN), F32),
            jax.ShapeDtypeStruct((NSRC, 16, COUT), BF16),
        ),
        in_specs=[hbm] * 6,
        out_specs=(hbm, hbm),
        scratch_shapes=[
            pltpu.VMEM((PIX, CIN), BF16),
            pltpu.VMEM((9, CIN, COUT), BF16),
            pltpu.VMEM((ROWS, 1, COLS), jnp.int32),
            pltpu.VMEM((ROWS, 1, COLS), jnp.int32),
            pltpu.VMEM((1, COUT), F32),
            pltpu.VMEM((NCLS, COUT), BF16),
            pltpu.VMEM((4 * PIX, QUARTER), BF16),
            pltpu.VMEM((COUT, COUT), F32),
            pltpu.VMEM((2, PIX, COUT), F32),
            pltpu.VMEM((2, PIX, COUT), F32),
            pltpu.VMEM((3, 6 * PIX, COUT), BF16),
            pltpu.VMEM((2, NX, 192, COUT), BF16),
            pltpu.VMEM((2, NX - 1, 192, COUT), BF16),
            pltpu.VMEM((2, 192, COUT), BF16),
            pltpu.VMEM((2, NY, 48, COUT), BF16),
            pltpu.VMEM((NX, 64, COUT), BF16),
            pltpu.VMEM((NX - 1, 64, COUT), BF16),
            pltpu.VMEM((64, COUT), BF16),
            pltpu.VMEM((NY, 16, COUT), BF16),
            pltpu.VMEM((4, 128, COUT), BF16),
            pltpu.VMEM((NY, 128, COUT), BF16),
            pltpu.VMEM((NX, 32, COUT), BF16),
            pltpu.VMEM((NX - 1, 32, COUT), BF16),
            pltpu.VMEM((160, COUT), F32),
            pltpu.VMEM((BANDS, 16, COUT), BF16),
            pltpu.VMEM((PIX, CIN), F32),
            dma((8,)), dma((4,)), dma((2,)), dma((2,)), dma((4,)), dma((4,)), dma((4,)), dma((2,)), dma((6,)),
            dma((3, 3)), dma((3, 3)), dma((3, 4)), dma((3, NY)),
            dma((4,)), dma((NY,)), dma((3,)), dma((3,)), dma((BANDS,)), dma((NSRC,)),
        ],
        compiler_params=pltpu.CompilerParams(
            collective_id=0, has_side_effects=True, vmem_limit_bytes=VMEM_LIMIT),
        name="step",
    )(
        image, taps, labels.transpose(1, 0, 2), pixel_weight.transpose(1, 0, 2),
        conv_bias.reshape(1, COUT), class_weight.T,
    )
    feature_grad, weight_grad = pl.pallas_call(
        write_kernel,
        out_shape=(
            jax.ShapeDtypeStruct((PIX, CIN), F32),
            jax.ShapeDtypeStruct((12, COUT), F32),
        ),
        in_specs=[hbm] * 2,
        out_specs=(hbm, hbm),
        scratch_shapes=[
            pltpu.VMEM((PIX, CIN), F32),
            pltpu.VMEM((NSRC, 16, COUT), BF16),
            pltpu.VMEM((12, COUT), F32),
            dma((WRITES + 1,)), dma((WRITES + 1,)),
        ],
        compiler_params=pltpu.CompilerParams(vmem_limit_bytes=VMEM_LIMIT),
        name="write",
    )(feature_grad, pieces)
    return feature_grad.reshape(features.shape), weight_grad


def solution(mesh):
    placed = (
        P("dp", "space", None, None),
        P("dp", "space", None),
        P("dp", "space", None),
        P(),
        P(),
        P(),
    )
    return jax.shard_map(
        on_device,
        mesh=mesh,
        in_specs=placed,
        out_specs=(P("dp", "space", None, None), P(("dp", "space"), None)),
        check_vma=False,
    )
```
